128 devices in a mesh: req: 4 (over z), seq: 32 (over y, x, core).
Axes of the slice: x: 4, y: 4, z: 4, core: 2. Of those that a mesh axis runs over, the one named last changes fastest.
Arguments:
- prompts: bfloat16 [24, 2048, 1024], P('req', 'seq'), may hold values from -6 to 6
- perm: int32 [24], replicated, may hold values from 0 to 23, each once
- lengths: int32 [24], replicated, may hold values from 512 to 2048, as said below
- norm_attn: float32 [1024], replicated, may hold values from 0.25 to 1.75
- norm_mlp: float32 [1024], replicated, may hold values from 0.25 to 1.75
- qkv_train: float32 [1024, 3072], P('seq', 'req'), may hold values from -0.1875 to 0.1875
- qkv_bias: float32 [3072], replicated, may hold values from -3 to 3
- out_train: float32 [1024, 1024], P('seq', 'req'), may hold values from -0.1875 to 0.1875
- gateup_train: float32 [1024, 5632], P('seq', 'req'), may hold values from -0.1875 to 0.1875
- down_train: float32 [2816, 1024], P('seq', 'req'), may hold values from -0.109375 to 0.109375
Outputs:
- states: bfloat16 [24, 2048, 1024], P('req', 'seq')
- key_cache: bfloat16 [24, 2048, 1024], P('req', 'seq')
- value_cache: bfloat16 [24, 2048, 1024], P('req', 'seq')
The draws below stay inside these ranges and needn't reach their ends.
Inputs may be any that keep to these rules, and one draw needn't show every extreme that they name: Valid lengths; some prompt has exactly 2048 and some exactly 512.
All inputs are finite; a program needn't handle non-finite values.
Results may differ from the reference program's by a relative error of at most 0.0085.
Values may be sent and summed in bfloat16 or wider, within the bound.
A program may use at most 192 MiB of HBM per device.

```python
import jax
import jax.numpy as jnp
from jax import lax

D = 1024
HEADS = 16
HD = 64
FF = 2816
LEN = 2048
PROMPTS = 24


def draw_lengths(key, part):
    first, second = jax.random.split(jax.random.fold_in(key, 17))
    base = jax.random.randint(first, (PROMPTS,), LEN // 4, LEN + 1)
    order = jax.random.permutation(second, PROMPTS)
    base = base.at[order[0]].set(LEN)
    base = base.at[order[1]].set(LEN // 4)
    return base.astype(jnp.int32)


def level_of(rng, extent, pieces, smallest, top_value):
    level, own = 1.0, jax.random.fold_in(rng, 6)
    for dim, blocks in pieces:
        steps = jnp.exp(jax.random.uniform(jax.random.fold_in(own, dim), (blocks,), jnp.float32, smallest / len(pieces), top_value / len(pieces)))
        level = level * jnp.repeat(steps, extent[dim] // blocks).reshape([-1 if axis == dim else 1 for axis in range(len(extent))])
    return level


def scatter_about(rng, dims, deviation, bound, shards=(), kind=jnp.bfloat16):
    factor_of = level_of(rng, dims, shards, -0.22, 0.18) if shards else 1.0
    entries = jax.random.normal(rng, dims, jnp.float32) * deviation * factor_of
    return jnp.minimum(jnp.maximum(entries, -bound), bound).astype(kind)


def setup_inputs(seed: int = 0) -> dict:
    seeds = jax.random.split(jax.random.key(seed), 11)
    return {
        "prompts": scatter_about(seeds[0], (PROMPTS, LEN, D), 1.0, 6.0, ((0, 4), (1, 32))),
        "perm": jax.random.permutation(seeds[1], PROMPTS).astype(jnp.int32),
        "lengths": draw_lengths(jax.random.fold_in(seeds[10], 71), 0),
        "norm_attn": jnp.clip(1.0 + 0.15 * jax.random.normal(seeds[3], (D,), jnp.float32), 0.25, 1.75),
        "norm_mlp": jnp.clip(1.0 + 0.15 * jax.random.normal(seeds[4], (D,), jnp.float32), 0.25, 1.75),
        "qkv_train": scatter_about(seeds[5], (D, 3 * D), D ** -0.5, 0.1875, ((0, 32), (1, 4)), jnp.float32),
        "qkv_bias": scatter_about(seeds[6], (3 * D,), 0.5, 3.0, (), jnp.float32),
        "out_train": scatter_about(seeds[7], (D, D), D ** -0.5, 0.1875, ((0, 32), (1, 4)), jnp.float32),
        "gateup_train": scatter_about(seeds[8], (D, 2 * FF), D ** -0.5, 0.1875, ((0, 32), (1, 4)), jnp.float32),
        "down_train": scatter_about(seeds[9], (FF, D), FF ** -0.5, 0.109375, ((0, 32), (1, 4)), jnp.float32),
    }


def rms_scale(rows, gain):
    rows = rows.astype(jnp.float32)
    return rows * lax.rsqrt(lax.optimization_barrier(jnp.mean(rows * rows, axis=-1, keepdims=True)) + 1e-06) * gain

def rotate(block, positions):
    half = HD // 2
    count = block.shape[0]
    freqs = jnp.power(1000000.0, -2.0 * jnp.arange(half).astype(jnp.float32) / HD)
    angle = positions[:, None] * freqs[None, :]
    cosine = jnp.cos(angle)[:, None, :]
    sine = jnp.sin(angle)[:, None, :]
    heads = block.reshape(count, -1, HD)
    first = heads[:, :, :half]
    second = heads[:, :, half:]
    turned = jnp.concatenate([first * cosine - second * sine, second * cosine + first * sine], axis=-1)
    return turned.reshape(count, -1)

def attend_one(items):
    query, keys, values = items
    query = query.reshape(LEN, HEADS, HD).astype(jnp.float32)
    keys = keys.reshape(LEN, HEADS, HD).astype(jnp.float32)
    values = values.reshape(LEN, HEADS, HD).astype(jnp.float32)
    scores = jnp.einsum('ihd,jhd->hij', query, keys) * HD ** (-0.5)
    causal = jnp.arange(LEN)[None, :] <= jnp.arange(LEN)[:, None]
    scores = jnp.where(causal[None], scores, -1e+30)
    top = lax.optimization_barrier(jnp.max(scores, axis=-1, keepdims=True))
    expo = jnp.exp(scores - top)
    probs = (expo / lax.optimization_barrier(jnp.sum(expo, axis=-1, keepdims=True))).astype(jnp.bfloat16)
    out = jnp.einsum('hij,jhd->ihd', probs.astype(jnp.float32), values)
    return out.astype(jnp.bfloat16).reshape(LEN, D)

def reference(prompts, perm, lengths, norm_attn, norm_mlp, qkv_train, qkv_bias, out_train, gateup_train, down_train):
    dealt = prompts[perm]
    slot_len = lengths[perm]
    valid = (jnp.arange(LEN, dtype=jnp.int32)[None, :] < slot_len[:, None]).astype(jnp.float32)
    rows = dealt.reshape(PROMPTS * LEN, D)
    positions = jnp.tile(jnp.arange(LEN, dtype=jnp.int32), PROMPTS).astype(jnp.float32)
    normed = rms_scale(rows, norm_attn).astype(jnp.bfloat16)
    qkv = jnp.dot(normed, qkv_train.astype(jnp.bfloat16), preferred_element_type=jnp.float32) + qkv_bias
    query = rotate(qkv[:, :D], positions).astype(jnp.bfloat16).reshape(PROMPTS, LEN, D)
    keys = rotate(qkv[:, D:2 * D], positions).astype(jnp.bfloat16).reshape(PROMPTS, LEN, D)
    values = qkv[:, 2 * D:].astype(jnp.bfloat16).reshape(PROMPTS, LEN, D)
    keep = valid.astype(jnp.bfloat16)[:, :, None]
    key_cache = keys * keep
    value_cache = values * keep
    attended = lax.map(attend_one, (query, keys, values)).reshape(PROMPTS * LEN, D)
    mid = rows.astype(jnp.float32) + jnp.dot(attended, out_train.astype(jnp.bfloat16), preferred_element_type=jnp.float32)
    normed2 = rms_scale(mid, norm_mlp).astype(jnp.bfloat16)
    both = jnp.dot(normed2, gateup_train.astype(jnp.bfloat16), preferred_element_type=jnp.float32)
    hidden = (jax.nn.silu(both[:, :FF]) * both[:, FF:]).astype(jnp.bfloat16)
    final = mid + jnp.dot(hidden, down_train.astype(jnp.bfloat16), preferred_element_type=jnp.float32)
    final = (final * valid.reshape(PROMPTS * LEN, 1)).astype(jnp.bfloat16).reshape(PROMPTS, LEN, D)
    inverse = jnp.argsort(perm).astype(jnp.int32)
    states = final[inverse]
    return (states, key_cache, value_cache)
```

```python
import jax
import jax.numpy as jnp
from jax import lax
from jax.sharding import PartitionSpec as P

HEADS = 16
HD = 64


def rms_scale(rows, gain):
    rows = rows.astype(jnp.float32)
    return rows * lax.rsqrt(jnp.mean(rows * rows, axis=-1, keepdims=True) + 1e-06) * gain


def rotate(block, positions):
    half = HD // 2
    count = block.shape[0]
    freqs = jnp.power(1000000.0, -2.0 * jnp.arange(half).astype(jnp.float32) / HD)
    angle = positions[:, None] * freqs[None, :]
    cosine = jnp.cos(angle)[:, None, :]
    sine = jnp.sin(angle)[:, None, :]
    heads = block.reshape(count, -1, HD)
    first = heads[:, :, :half]
    second = heads[:, :, half:]
    turned = jnp.concatenate(
        [first * cosine - second * sine, second * cosine + first * sine], axis=-1
    )
    return turned.reshape(count, -1)


def apply(inputs, gathered):
    out = jnp.einsum("ik,rkn->irn", inputs, gathered, preferred_element_type=jnp.float32)
    return out.reshape(inputs.shape[0], -1)


def attend(items):
    query, keys, values = items
    length = query.shape[2]
    block = min(512, length)
    scale = HD ** (-0.5)
    pieces = []
    for start in range(0, length, block):
        q_block = query[:, :, start : start + block]
        scores = (
            jnp.einsum("bnid,bnjd->bnij", q_block, keys, preferred_element_type=jnp.float32) * scale
        )
        causal = jnp.arange(length)[None, :] <= (start + jnp.arange(block))[:, None]
        scores = jnp.where(causal[None, None], scores, -1e30)
        top = jnp.max(scores, axis=-1, keepdims=True)
        expo = jnp.exp(scores - top)
        probs = (expo / jnp.sum(expo, axis=-1, keepdims=True)).astype(jnp.bfloat16)
        out = jnp.einsum("bnij,bnjd->bnid", probs, values, preferred_element_type=jnp.float32)
        pieces.append(out.astype(jnp.bfloat16))
    return jnp.concatenate(pieces, axis=2)


def gather_weights(pieces, after=None):
    flat = jnp.concatenate([p.astype(jnp.bfloat16).reshape(-1) for p in pieces])
    if after is not None:
        flat, _ = lax.optimization_barrier((flat, after))
    return lax.all_gather(flat[None], ("req", "seq"), axis=0, tiled=True)


def local(
    prompts,
    perm,
    lengths,
    norm_attn,
    norm_mlp,
    qkv_train,
    qkv_bias,
    out_train,
    gateup_train,
    down_train,
):
    count = prompts.shape[0]
    tok = prompts.shape[1]
    width = prompts.shape[2]
    groups = lax.axis_size("seq")
    blocks = lax.axis_size("req")

    attn_w = gather_weights([qkv_train, out_train])
    mlp_w = gather_weights([gateup_train, down_train])
    qkv_size = qkv_train.size
    gu_size = gateup_train.size
    w_qkv = attn_w[:, :qkv_size].reshape(blocks, -1, qkv_train.shape[1])
    w_out = attn_w[:, qkv_size:].reshape(blocks, -1, out_train.shape[1])
    w_gu = mlp_w[:, :gu_size].reshape(blocks, -1, gateup_train.shape[1])
    w_down = mlp_w[:, gu_size:].reshape(blocks, -1, down_train.shape[1])

    places = lax.axis_index("seq") * tok + jnp.arange(tok, dtype=jnp.int32)
    positions = jnp.tile(places, count).astype(jnp.float32)

    initials = lax.axis_index("req") * count + jnp.arange(count, dtype=jnp.int32)
    own_len = jnp.take(lengths, initials)
    valid = (places[None, :] < own_len[:, None]).astype(jnp.float32).reshape(count * tok, 1)
    rows = prompts.reshape(count * tok, width)
    normed = rms_scale(rows, norm_attn).astype(jnp.bfloat16)
    qkv = apply(normed, w_qkv) + qkv_bias
    query = rotate(qkv[:, :width], positions).astype(jnp.bfloat16)
    keys = rotate(qkv[:, width : 2 * width], positions).astype(jnp.bfloat16)
    values = qkv[:, 2 * width :].astype(jnp.bfloat16)
    per_device = count * HEADS // groups

    def to_pairs(array):
        paired = array.reshape(count, tok, HEADS, HD).transpose(0, 2, 1, 3)
        return paired.reshape(groups, per_device, tok, HD)

    gathered = attend(
        (
            lax.all_to_all(to_pairs(query), "seq", split_axis=0, concat_axis=2, tiled=True),
            lax.all_to_all(to_pairs(keys), "seq", split_axis=0, concat_axis=2, tiled=True),
            lax.all_to_all(to_pairs(values), "seq", split_axis=0, concat_axis=2, tiled=True),
        )
    )
    returned = lax.all_to_all(gathered, "seq", split_axis=2, concat_axis=0, tiled=True)
    attended = (
        returned.reshape(count, HEADS, tok, HD).transpose(0, 2, 1, 3).reshape(count * tok, width)
    )
    mid = rows.astype(jnp.float32) + apply(attended, w_out)
    normed2 = rms_scale(mid, norm_mlp).astype(jnp.bfloat16)
    both = apply(normed2, w_gu)
    half = both.shape[1] // 2
    hidden = (jax.nn.silu(both[:, :half]) * both[:, half:]).astype(jnp.bfloat16)
    states = (
        ((mid + apply(hidden, w_down)) * valid).astype(jnp.bfloat16).reshape(count, tok, width)
    )

    later, _ = lax.optimization_barrier((prompts, qkv))
    everyone = lax.all_gather(later, "req", axis=0, tiled=True)
    everyone, _ = lax.optimization_barrier((everyone, hidden))
    chosen = jnp.take(perm, initials)
    dealt = jnp.take(everyone, chosen, axis=0).reshape(count * tok, width)
    slot_len = jnp.take(lengths, chosen)
    keep = (places[None, :] < slot_len[:, None]).astype(jnp.bfloat16).reshape(count * tok, 1)
    normed_d = rms_scale(dealt, norm_attn).astype(jnp.bfloat16)
    qkv_d = apply(normed_d, w_qkv) + qkv_bias
    keys_d = rotate(qkv_d[:, width : 2 * width], positions).astype(jnp.bfloat16)
    values_d = qkv_d[:, 2 * width :].astype(jnp.bfloat16)
    key_cache = (keys_d * keep).reshape(count, tok, width)
    value_cache = (values_d * keep).reshape(count, tok, width)
    return (states, key_cache, value_cache)


def solution(mesh):
    placed = (
        P("req", "seq", None),
        P(),
        P(),
        P(),
        P(),
        P("seq", "req"),
        P(),
        P("seq", "req"),
        P("seq", "req"),
        P("seq", "req"),
    )
    return jax.shard_map(
        local,
        mesh=mesh,
        in_specs=placed,
        out_specs=(P("req", "seq", None), P("req", "seq", None), P("req", "seq", None)),
        check_vma=False,
    )
```

```python
import jax
import jax.numpy as jnp
from jax import lax
from jax.sharding import PartitionSpec as P

HEADS = 16
HD = 64


def rms_scale(rows, gain):
    rows = rows.astype(jnp.float32)
    return rows * lax.rsqrt(jnp.mean(rows * rows, axis=-1, keepdims=True) + 1e-06) * gain


def rotate(block, positions):
    half = HD // 2
    count = block.shape[0]
    freqs = jnp.power(1000000.0, -2.0 * jnp.arange(half).astype(jnp.float32) / HD)
    angle = positions[:, None] * freqs[None, :]
    cosine = jnp.cos(angle)[:, None, :]
    sine = jnp.sin(angle)[:, None, :]
    heads = block.reshape(count, -1, HD)
    first = heads[:, :, :half]
    second = heads[:, :, half:]
    turned = jnp.concatenate(
        [first * cosine - second * sine, second * cosine + first * sine], axis=-1
    )
    return turned.reshape(count, -1)


def apply(inputs, gathered):
    out = jnp.einsum("ik,rkn->irn", inputs, gathered, preferred_element_type=jnp.float32)
    return out.reshape(inputs.shape[0], -1)


def attend(items):
    query, keys, values = items
    length = query.shape[2]
    block = min(512, length)
    scale = HD ** (-0.5)
    pieces = []
    for start in range(0, length, block):
        q_block = query[:, :, start : start + block]
        scores = (
            jnp.einsum("bnid,bnjd->bnij", q_block, keys, preferred_element_type=jnp.float32) * scale
        )
        causal = jnp.arange(length)[None, :] <= (start + jnp.arange(block))[:, None]
        scores = jnp.where(causal[None, None], scores, -1e30)
        top = jnp.max(scores, axis=-1, keepdims=True)
        expo = jnp.exp(scores - top)
        probs = (expo / jnp.sum(expo, axis=-1, keepdims=True)).astype(jnp.bfloat16)
        out = jnp.einsum("bnij,bnjd->bnid", probs, values, preferred_element_type=jnp.float32)
        pieces.append(out.astype(jnp.bfloat16))
    return jnp.concatenate(pieces, axis=2)


def gather_weights(piece, rows=None):
    piece = piece.astype(jnp.bfloat16)
    if rows is not None and rows != piece.shape[0]:
        piece = jnp.pad(piece, ((0, rows - piece.shape[0]), (0, 0)))
    whole = lax.all_gather(piece[None], ("req", "seq"), axis=0, tiled=True)
    return whole.reshape(lax.axis_size("req"), -1, piece.shape[1])


def local(
    prompts,
    perm,
    lengths,
    norm_attn,
    norm_mlp,
    qkv_train,
    qkv_bias,
    out_train,
    gateup_train,
    down_train,
):
    count = prompts.shape[0]
    tok = prompts.shape[1]
    width = prompts.shape[2]
    groups = lax.axis_size("seq")

    w_qkv = gather_weights(qkv_train)
    w_out = gather_weights(out_train)
    w_gu = gather_weights(gateup_train)
    down_rows = down_train.shape[0]
    padded_rows = -(-down_rows // 16) * 16
    w_down = gather_weights(down_train, padded_rows)

    places = lax.axis_index("seq") * tok + jnp.arange(tok, dtype=jnp.int32)
    positions = jnp.tile(places, count).astype(jnp.float32)

    initials = lax.axis_index("req") * count + jnp.arange(count, dtype=jnp.int32)
    own_len = jnp.take(lengths, initials)
    valid = (places[None, :] < own_len[:, None]).astype(jnp.float32).reshape(count * tok, 1)
    rows = prompts.reshape(count * tok, width)
    normed = rms_scale(rows, norm_attn).astype(jnp.bfloat16)
    qkv = apply(normed, w_qkv) + qkv_bias
    query = rotate(qkv[:, :width], positions).astype(jnp.bfloat16)
    keys = rotate(qkv[:, width : 2 * width], positions).astype(jnp.bfloat16)
    values = qkv[:, 2 * width :].astype(jnp.bfloat16)
    per_device = count * HEADS // groups

    def to_pairs(array):
        paired = array.reshape(count, tok, HEADS, HD).transpose(0, 2, 1, 3)
        return paired.reshape(groups, per_device, tok, HD)

    gathered = attend(
        (
            lax.all_to_all(to_pairs(query), "seq", split_axis=0, concat_axis=2, tiled=True),
            lax.all_to_all(to_pairs(keys), "seq", split_axis=0, concat_axis=2, tiled=True),
            lax.all_to_all(to_pairs(values), "seq", split_axis=0, concat_axis=2, tiled=True),
        )
    )
    returned = lax.all_to_all(gathered, "seq", split_axis=2, concat_axis=0, tiled=True)
    attended = (
        returned.reshape(count, HEADS, tok, HD).transpose(0, 2, 1, 3).reshape(count * tok, width)
    )
    mid = rows.astype(jnp.float32) + apply(attended, w_out)
    normed2 = rms_scale(mid, norm_mlp).astype(jnp.bfloat16)
    both = apply(normed2, w_gu)
    half = both.shape[1] // 2
    hidden = (jax.nn.silu(both[:, :half]) * both[:, half:]).astype(jnp.bfloat16)
    hidden = jnp.pad(
        hidden.reshape(count * tok, groups, down_rows), ((0, 0), (0, 0), (0, padded_rows - down_rows))
    ).reshape(count * tok, -1)
    states = (
        ((mid + apply(hidden, w_down)) * valid).astype(jnp.bfloat16).reshape(count, tok, width)
    )

    later, _ = lax.optimization_barrier((prompts, qkv))
    everyone = lax.all_gather(later, "req", axis=0, tiled=True)
    everyone, _ = lax.optimization_barrier((everyone, hidden))
    chosen = jnp.take(perm, initials)
    dealt = jnp.take(everyone, chosen, axis=0).reshape(count * tok, width)
    slot_len = jnp.take(lengths, chosen)
    keep = (places[None, :] < slot_len[:, None]).astype(jnp.bfloat16).reshape(count * tok, 1)
    normed_d = rms_scale(dealt, norm_attn).astype(jnp.bfloat16)
    qkv_d = apply(normed_d, w_qkv) + qkv_bias
    keys_d = rotate(qkv_d[:, width : 2 * width], positions).astype(jnp.bfloat16)
    values_d = qkv_d[:, 2 * width :].astype(jnp.bfloat16)
    key_cache = (keys_d * keep).reshape(count, tok, width)
    value_cache = (values_d * keep).reshape(count, tok, width)
    return (states, key_cache, value_cache)


def solution(mesh):
    placed = (
        P("req", "seq", None),
        P(),
        P(),
        P(),
        P(),
        P("seq", "req"),
        P(),
        P("seq", "req"),
        P("seq", "req"),
        P("seq", "req"),
    )
    return jax.shard_map(
        local,
        mesh=mesh,
        in_specs=placed,
        out_specs=(P("req", "seq", None), P("req", "seq", None), P("req", "seq", None)),
        check_vma=False,
    )
```

```python
import jax
import jax.numpy as jnp
from jax import lax
from jax.sharding import PartitionSpec as P

HEADS = 16
HD = 64


def rms_scale(rows, gain):
    rows = rows.astype(jnp.float32)
    return rows * lax.rsqrt(jnp.mean(rows * rows, axis=-1, keepdims=True) + 1e-06) * gain


def rotate(block, positions):
    half = HD // 2
    count = block.shape[0]
    freqs = jnp.power(1000000.0, -2.0 * jnp.arange(half).astype(jnp.float32) / HD)
    angle = positions[:, None] * freqs[None, :]
    cosine = jnp.cos(angle)[:, None, :]
    sine = jnp.sin(angle)[:, None, :]
    heads = block.reshape(count, -1, HD)
    first = heads[:, :, :half]
    second = heads[:, :, half:]
    turned = jnp.concatenate(
        [first * cosine - second * sine, second * cosine + first * sine], axis=-1
    )
    return turned.reshape(count, -1)


def apply(inputs, gathered):
    return jnp.concatenate(
        [jnp.dot(inputs, gathered[r], preferred_element_type=jnp.float32) for r in range(gathered.shape[0])],
        axis=1,
    )


def attend(items):
    query, keys, values = items
    length = query.shape[2]
    block = min(512, length)
    scale = HD ** (-0.5)
    pieces = []
    for start in range(0, length, block):
        q_block = query[:, :, start : start + block]
        scores = (
            jnp.einsum("bnid,bnjd->bnij", q_block, keys, preferred_element_type=jnp.float32) * scale
        )
        causal = jnp.arange(length)[None, :] <= (start + jnp.arange(block))[:, None]
        scores = jnp.where(causal[None, None], scores, -1e30)
        top = jnp.max(scores, axis=-1, keepdims=True)
        expo = jnp.exp(scores - top)
        probs = (expo / jnp.sum(expo, axis=-1, keepdims=True)).astype(jnp.bfloat16)
        out = jnp.einsum("bnij,bnjd->bnid", probs, values, preferred_element_type=jnp.float32)
        pieces.append(out.astype(jnp.bfloat16))
    return jnp.concatenate(pieces, axis=2)


def gather_weights(piece, rows=None):
    piece = piece.astype(jnp.bfloat16)
    if rows is not None and rows != piece.shape[0]:
        piece = jnp.pad(piece, ((0, rows - piece.shape[0]), (0, 0)))
    whole = lax.all_gather(piece[None], ("req", "seq"), axis=0, tiled=True)
    return whole.reshape(lax.axis_size("req"), -1, piece.shape[1])


def local(
    prompts,
    perm,
    lengths,
    norm_attn,
    norm_mlp,
    qkv_train,
    qkv_bias,
    out_train,
    gateup_train,
    down_train,
):
    count = prompts.shape[0]
    tok = prompts.shape[1]
    width = prompts.shape[2]
    groups = lax.axis_size("seq")

    w_qkv = gather_weights(qkv_train)
    down_rows = down_train.shape[0]
    padded_rows = -(-down_rows // 16) * 16
    width_rows = out_train.shape[0]
    down_piece = jnp.pad(down_train.astype(jnp.bfloat16), ((0, padded_rows - down_rows), (0, 0)))
    side = jnp.concatenate(
        [out_train.astype(jnp.bfloat16), gateup_train.astype(jnp.bfloat16), down_piece.reshape(width_rows, -1)],
        axis=1,
    )
    rest = lax.all_gather(side[None], ("req", "seq"), axis=0, tiled=True)
    blocks = lax.axis_size("req")
    cut_out = out_train.shape[1]
    cut_gu = cut_out + gateup_train.shape[1]
    w_out = rest[:, :, :cut_out].reshape(blocks, -1, cut_out)
    w_gu = rest[:, :, cut_out:cut_gu].reshape(blocks, -1, gateup_train.shape[1])
    w_down = rest[:, :, cut_gu:].reshape(blocks, -1, down_train.shape[1])

    places = lax.axis_index("seq") * tok + jnp.arange(tok, dtype=jnp.int32)
    positions = jnp.tile(places, count).astype(jnp.float32)

    initials = lax.axis_index("req") * count + jnp.arange(count, dtype=jnp.int32)
    own_len = jnp.take(lengths, initials)
    valid = (places[None, :] < own_len[:, None]).astype(jnp.float32).reshape(count * tok, 1)
    rows = prompts.reshape(count * tok, width)
    normed = rms_scale(rows, norm_attn).astype(jnp.bfloat16)
    qkv = apply(normed, w_qkv) + qkv_bias
    query = rotate(qkv[:, :width], positions).astype(jnp.bfloat16)
    keys = rotate(qkv[:, width : 2 * width], positions).astype(jnp.bfloat16)
    values = qkv[:, 2 * width :].astype(jnp.bfloat16)
    per_device = count * HEADS // groups

    def to_pairs(array):
        paired = array.reshape(count, tok, HEADS, HD).transpose(0, 2, 1, 3)
        return paired.reshape(groups, per_device, tok, HD)

    gathered = attend(
        (
            lax.all_to_all(to_pairs(query), "seq", split_axis=0, concat_axis=2, tiled=True),
            lax.all_to_all(to_pairs(keys), "seq", split_axis=0, concat_axis=2, tiled=True),
            lax.all_to_all(to_pairs(values), "seq", split_axis=0, concat_axis=2, tiled=True),
        )
    )
    returned = lax.all_to_all(gathered, "seq", split_axis=2, concat_axis=0, tiled=True)
    attended = (
        returned.reshape(count, HEADS, tok, HD).transpose(0, 2, 1, 3).reshape(count * tok, width)
    )
    mid = rows.astype(jnp.float32) + apply(attended, w_out)
    normed2 = rms_scale(mid, norm_mlp).astype(jnp.bfloat16)
    both = apply(normed2, w_gu)
    half = both.shape[1] // 2
    hidden = (jax.nn.silu(both[:, :half]) * both[:, half:]).astype(jnp.bfloat16)
    hidden = jnp.pad(
        hidden.reshape(count * tok, groups, down_rows), ((0, 0), (0, 0), (0, padded_rows - down_rows))
    ).reshape(count * tok, -1)
    states = (
        ((mid + apply(hidden, w_down)) * valid).astype(jnp.bfloat16).reshape(count, tok, width)
    )

    later, _ = lax.optimization_barrier((prompts, qkv))
    everyone = lax.all_gather(later, "req", axis=0, tiled=True)
    everyone, _ = lax.optimization_barrier((everyone, hidden))
    chosen = jnp.take(perm, initials)
    dealt = jnp.take(everyone, chosen, axis=0).reshape(count * tok, width)
    slot_len = jnp.take(lengths, chosen)
    keep = (places[None, :] < slot_len[:, None]).astype(jnp.bfloat16).reshape(count * tok, 1)
    normed_d = rms_scale(dealt, norm_attn).astype(jnp.bfloat16)
    qkv_d = apply(normed_d, w_qkv) + qkv_bias
    keys_d = rotate(qkv_d[:, width : 2 * width], positions).astype(jnp.bfloat16)
    values_d = qkv_d[:, 2 * width :].astype(jnp.bfloat16)
    key_cache = (keys_d * keep).reshape(count, tok, width)
    value_cache = (values_d * keep).reshape(count, tok, width)
    return (states, key_cache, value_cache)


def solution(mesh):
    placed = (
        P("req", "seq", None),
        P(),
        P(),
        P(),
        P(),
        P("seq", "req"),
        P(),
        P("seq", "req"),
        P("seq", "req"),
        P("seq", "req"),
    )
    return jax.shard_map(
        local,
        mesh=mesh,
        in_specs=placed,
        out_specs=(P("req", "seq", None), P("req", "seq", None), P("req", "seq", None)),
        check_vma=False,
    )
```

```python
import jax
import jax.numpy as jnp
from jax import lax
from jax.sharding import PartitionSpec as P
from jax.experimental import pallas as pl
from jax.experimental.pallas import tpu as pltpu

HEADS = 16
HD = 64


def rms_scale(rows, gain):
    rows = rows.astype(jnp.float32)
    return rows * lax.rsqrt(jnp.mean(rows * rows, axis=-1, keepdims=True) + 1e-06) * gain


def rotate(block, positions):
    half = HD // 2
    count = block.shape[0]
    freqs = jnp.power(1000000.0, -2.0 * jnp.arange(half).astype(jnp.float32) / HD)
    angle = positions[:, None] * freqs[None, :]
    cosine = jnp.cos(angle)[:, None, :]
    sine = jnp.sin(angle)[:, None, :]
    heads = block.reshape(count, -1, HD)
    first = heads[:, :, :half]
    second = heads[:, :, half:]
    turned = jnp.concatenate(
        [first * cosine - second * sine, second * cosine + first * sine], axis=-1
    )
    return turned.reshape(count, -1)


def apply(inputs, gathered):
    return jnp.concatenate(
        [jnp.dot(inputs, gathered[r], preferred_element_type=jnp.float32) for r in range(gathered.shape[0])],
        axis=1,
    )


Q_ROWS = 256
K_ROWS = 256


def attention_kernel(q_ref, k_ref, v_ref, o_ref):
    block = pl.program_id(1)
    query = q_ref[...].reshape(Q_ROWS, HD)
    scale = HD ** (-0.5)
    rows = block * Q_ROWS + lax.broadcasted_iota(jnp.int32, (Q_ROWS, K_ROWS), 0)
    steps = (block + 1) * (Q_ROWS // K_ROWS)

    def scores(step):
        keys = k_ref[pl.ds(step * (K_ROWS // 64), K_ROWS // 64)].reshape(K_ROWS, HD)
        raw = lax.dot_general(query, keys, (((1,), (1,)), ((), ())), preferred_element_type=jnp.float32)
        cols = step * K_ROWS + lax.broadcasted_iota(jnp.int32, (Q_ROWS, K_ROWS), 1)
        return jnp.where(cols <= rows, raw * scale, -1e30)

    def first(step, carry):
        top, total = carry
        s = scores(step)
        new_top = jnp.maximum(top, jnp.max(s, axis=1, keepdims=True))
        total = total * jnp.exp(top - new_top) + jnp.sum(jnp.exp(s - new_top), axis=1, keepdims=True)
        return new_top, total

    top, total = lax.fori_loop(
        0,
        steps,
        first,
        (jnp.full((Q_ROWS, 1), -jnp.inf, jnp.float32), jnp.zeros((Q_ROWS, 1), jnp.float32)),
    )

    def second(step, acc):
        probs = (jnp.exp(scores(step) - top) / total).astype(jnp.bfloat16)
        values = v_ref[pl.ds(step * (K_ROWS // 64), K_ROWS // 64)].reshape(K_ROWS, HD)
        return acc + jnp.dot(probs, values, preferred_element_type=jnp.float32)

    acc = lax.fori_loop(0, steps, second, jnp.zeros((Q_ROWS, HD), jnp.float32))
    o_ref[...] = acc.astype(o_ref.dtype).reshape(o_ref.shape)


def attend(received):
    sources, _, pairs, tok, _ = received.shape
    per_block = Q_ROWS // tok
    return pl.pallas_call(
        attention_kernel,
        grid=(pairs, sources // per_block),
        in_specs=[
            pl.BlockSpec((per_block, None, None, tok, HD), lambda p, b: (b, 0, p, 0, 0)),
            pl.BlockSpec((sources, None, None, tok, HD), lambda p, b: (0, 1, p, 0, 0)),
            pl.BlockSpec((sources, None, None, tok, HD), lambda p, b: (0, 2, p, 0, 0)),
        ],
        out_specs=pl.BlockSpec((per_block, None, tok, HD), lambda p, b: (b, p, 0, 0)),
        out_shape=jax.ShapeDtypeStruct((sources, pairs, tok, HD), jnp.bfloat16),
        cost_estimate=pl.CostEstimate(
            flops=4 * pairs * sources * tok * sources * tok * HD // 2 * 2,
            transcendentals=2 * pairs * (sources * tok) ** 2 // 2,
            bytes_accessed=4 * pairs * sources * tok * HD * 2,
        ),
    )(received, received, received)


def gather_weights(piece, rows=None):
    piece = piece.astype(jnp.bfloat16)
    if rows is not None and rows != piece.shape[0]:
        piece = jnp.pad(piece, ((0, rows - piece.shape[0]), (0, 0)))
    whole = lax.all_gather(piece[None], ("req", "seq"), axis=0, tiled=True)
    return whole.reshape(lax.axis_size("req"), -1, piece.shape[1])


def local(
    prompts,
    perm,
    lengths,
    norm_attn,
    norm_mlp,
    qkv_train,
    qkv_bias,
    out_train,
    gateup_train,
    down_train,
):
    count = prompts.shape[0]
    tok = prompts.shape[1]
    width = prompts.shape[2]
    groups = lax.axis_size("seq")

    w_qkv = gather_weights(qkv_train)
    down_rows = down_train.shape[0]
    padded_rows = -(-down_rows // 16) * 16
    width_rows = out_train.shape[0]
    down_piece = jnp.pad(down_train.astype(jnp.bfloat16), ((0, padded_rows - down_rows), (0, 0)))
    side = jnp.concatenate(
        [out_train.astype(jnp.bfloat16), gateup_train.astype(jnp.bfloat16), down_piece.reshape(width_rows, -1)],
        axis=1,
    )
    rest = lax.all_gather(side[None], ("req", "seq"), axis=0, tiled=True)
    blocks = lax.axis_size("req")
    cut_out = out_train.shape[1]
    cut_gu = cut_out + gateup_train.shape[1]
    w_out = rest[:, :, :cut_out].reshape(blocks, -1, cut_out)
    w_gu = rest[:, :, cut_out:cut_gu].reshape(blocks, -1, gateup_train.shape[1])
    w_down = rest[:, :, cut_gu:].reshape(blocks, -1, down_train.shape[1])

    places = lax.axis_index("seq") * tok + jnp.arange(tok, dtype=jnp.int32)
    positions = jnp.tile(places, count).astype(jnp.float32)

    initials = lax.axis_index("req") * count + jnp.arange(count, dtype=jnp.int32)
    own_len = jnp.take(lengths, initials)
    valid = (places[None, :] < own_len[:, None]).astype(jnp.float32).reshape(count * tok, 1)
    rows = prompts.reshape(count * tok, width)
    normed = rms_scale(rows, norm_attn).astype(jnp.bfloat16)
    qkv = apply(normed, w_qkv) + qkv_bias
    query = rotate(qkv[:, :width], positions).astype(jnp.bfloat16)
    keys = rotate(qkv[:, width : 2 * width], positions).astype(jnp.bfloat16)
    values = qkv[:, 2 * width :].astype(jnp.bfloat16)
    per_device = count * HEADS // groups

    def to_pairs(array):
        paired = array.reshape(count, tok, HEADS, HD).transpose(0, 2, 1, 3)
        return paired.reshape(groups, 1, per_device, tok, HD)

    sent = jnp.concatenate([to_pairs(query), to_pairs(keys), to_pairs(values)], axis=1)
    received = lax.all_to_all(sent, "seq", split_axis=0, concat_axis=0, tiled=True)
    gathered = attend(received)
    returned = lax.all_to_all(gathered, "seq", split_axis=0, concat_axis=0, tiled=True)
    attended = (
        returned.reshape(count, HEADS, tok, HD).transpose(0, 2, 1, 3).reshape(count * tok, width)
    )
    mid = rows.astype(jnp.float32) + apply(attended, w_out)
    normed2 = rms_scale(mid, norm_mlp).astype(jnp.bfloat16)
    both = apply(normed2, w_gu)
    half = both.shape[1] // 2
    hidden = (jax.nn.silu(both[:, :half]) * both[:, half:]).astype(jnp.bfloat16)
    hidden = jnp.pad(
        hidden.reshape(count * tok, groups, down_rows), ((0, 0), (0, 0), (0, padded_rows - down_rows))
    ).reshape(count * tok, -1)
    states = (
        ((mid + apply(hidden, w_down)) * valid).astype(jnp.bfloat16).reshape(count, tok, width)
    )

    later, _ = lax.optimization_barrier((prompts, qkv))
    everyone = lax.all_gather(later, "req", axis=0, tiled=True)
    everyone, _ = lax.optimization_barrier((everyone, hidden))
    chosen = jnp.take(perm, initials)
    dealt = jnp.take(everyone, chosen, axis=0).reshape(count * tok, width)
    slot_len = jnp.take(lengths, chosen)
    keep = (places[None, :] < slot_len[:, None]).astype(jnp.bfloat16).reshape(count * tok, 1)
    normed_d = rms_scale(dealt, norm_attn).astype(jnp.bfloat16)
    qkv_d = apply(normed_d, w_qkv) + qkv_bias
    keys_d = rotate(qkv_d[:, width : 2 * width], positions).astype(jnp.bfloat16)
    values_d = qkv_d[:, 2 * width :].astype(jnp.bfloat16)
    key_cache = (keys_d * keep).reshape(count, tok, width)
    value_cache = (values_d * keep).reshape(count, tok, width)
    return (states, key_cache, value_cache)


def solution(mesh):
    placed = (
        P("req", "seq", None),
        P(),
        P(),
        P(),
        P(),
        P("seq", "req"),
        P(),
        P("seq", "req"),
        P("seq", "req"),
        P("seq", "req"),
    )
    return jax.shard_map(
        local,
        mesh=mesh,
        in_specs=placed,
        out_specs=(P("req", "seq", None), P("req", "seq", None), P("req", "seq", None)),
        check_vma=False,
    )
```

```python
import jax
import jax.numpy as jnp
from jax import lax
from jax.sharding import PartitionSpec as P

HEADS = 16
HD = 64


def rms_scale(rows, gain):
    rows = rows.astype(jnp.float32)
    return rows * lax.rsqrt(jnp.mean(rows * rows, axis=-1, keepdims=True) + 1e-06) * gain


def rotate(block, positions):
    half = HD // 2
    count = block.shape[0]
    freqs = jnp.power(1000000.0, -2.0 * jnp.arange(half).astype(jnp.float32) / HD)
    angle = positions[:, None] * freqs[None, :]
    cosine = jnp.cos(angle)[:, None, :]
    sine = jnp.sin(angle)[:, None, :]
    heads = block.reshape(count, -1, HD)
    first = heads[:, :, :half]
    second = heads[:, :, half:]
    turned = jnp.concatenate(
        [first * cosine - second * sine, second * cosine + first * sine], axis=-1
    )
    return turned.reshape(count, -1)


def apply(inputs, gathered):
    out = jnp.einsum("ik,rkn->irn", inputs, gathered, preferred_element_type=jnp.float32)
    return out.reshape(inputs.shape[0], -1)


def attend_xla(items):
    query, keys, values = items
    length = query.shape[2]
    block = min(512, length)
    scale = HD ** (-0.5)
    pieces = []
    for start in range(0, length, block):
        q_block = query[:, :, start : start + block]
        scores = (
            jnp.einsum("bnid,bnjd->bnij", q_block, keys, preferred_element_type=jnp.float32) * scale
        )
        causal = jnp.arange(length)[None, :] <= (start + jnp.arange(block))[:, None]
        scores = jnp.where(causal[None, None], scores, -1e30)
        top = jnp.max(scores, axis=-1, keepdims=True)
        expo = jnp.exp(scores - top)
        probs = (expo / jnp.sum(expo, axis=-1, keepdims=True)).astype(jnp.bfloat16)
        out = jnp.einsum("bnij,bnjd->bnid", probs, values, preferred_element_type=jnp.float32)
        pieces.append(out.astype(jnp.bfloat16))
    return jnp.concatenate(pieces, axis=2)


def gather_weights(piece, rows=None):
    piece = piece.astype(jnp.bfloat16)
    if rows is not None and rows != piece.shape[0]:
        piece = jnp.pad(piece, ((0, rows - piece.shape[0]), (0, 0)))
    whole = lax.all_gather(piece[None], ("req", "seq"), axis=0, tiled=True)
    return whole.reshape(lax.axis_size("req"), -1, piece.shape[1])


def local(
    prompts,
    perm,
    lengths,
    norm_attn,
    norm_mlp,
    qkv_train,
    qkv_bias,
    out_train,
    gateup_train,
    down_train,
):
    count = prompts.shape[0]
    tok = prompts.shape[1]
    width = prompts.shape[2]
    groups = lax.axis_size("seq")

    w_qkv = gather_weights(qkv_train)
    down_rows = down_train.shape[0]
    padded_rows = -(-down_rows // 16) * 16
    width_rows = out_train.shape[0]
    down_piece = jnp.pad(down_train.astype(jnp.bfloat16), ((0, padded_rows - down_rows), (0, 0)))
    side = jnp.concatenate(
        [out_train.astype(jnp.bfloat16), gateup_train.astype(jnp.bfloat16), down_piece.reshape(width_rows, -1)],
        axis=1,
    )
    rest = lax.all_gather(side[None], ("req", "seq"), axis=0, tiled=True)
    blocks = lax.axis_size("req")
    cut_out = out_train.shape[1]
    cut_gu = cut_out + gateup_train.shape[1]
    w_out = rest[:, :, :cut_out].reshape(blocks, -1, cut_out)
    w_gu = rest[:, :, cut_out:cut_gu].reshape(blocks, -1, gateup_train.shape[1])
    w_down = rest[:, :, cut_gu:].reshape(blocks, -1, down_train.shape[1])

    places = lax.axis_index("seq") * tok + jnp.arange(tok, dtype=jnp.int32)
    positions = jnp.tile(places, count).astype(jnp.float32)

    initials = lax.axis_index("req") * count + jnp.arange(count, dtype=jnp.int32)
    own_len = jnp.take(lengths, initials)
    valid = (places[None, :] < own_len[:, None]).astype(jnp.float32).reshape(count * tok, 1)
    rows = prompts.reshape(count * tok, width)
    normed = rms_scale(rows, norm_attn).astype(jnp.bfloat16)
    qkv = apply(normed, w_qkv) + qkv_bias
    query = rotate(qkv[:, :width], positions).astype(jnp.bfloat16)
    keys = rotate(qkv[:, width : 2 * width], positions).astype(jnp.bfloat16)
    values = qkv[:, 2 * width :].astype(jnp.bfloat16)
    per_device = count * HEADS // groups

    def to_pairs(array):
        paired = array.reshape(count, tok, HEADS, HD).transpose(0, 2, 1, 3)
        return paired.reshape(groups, per_device, tok, HD)

    gathered = attend_xla(
        (
            lax.all_to_all(to_pairs(query), "seq", split_axis=0, concat_axis=2, tiled=True),
            lax.all_to_all(to_pairs(keys), "seq", split_axis=0, concat_axis=2, tiled=True),
            lax.all_to_all(to_pairs(values), "seq", split_axis=0, concat_axis=2, tiled=True),
        )
    )
    returned = lax.all_to_all(gathered, "seq", split_axis=2, concat_axis=0, tiled=True)
    attended = (
        returned.reshape(count, HEADS, tok, HD).transpose(0, 2, 1, 3).reshape(count * tok, width)
    )
    mid = rows.astype(jnp.float32) + apply(attended, w_out)
    normed2 = rms_scale(mid, norm_mlp).astype(jnp.bfloat16)
    both = apply(normed2, w_gu)
    half = both.shape[1] // 2
    hidden = (jax.nn.silu(both[:, :half]) * both[:, half:]).astype(jnp.bfloat16)
    hidden = jnp.pad(
        hidden.reshape(count * tok, groups, down_rows), ((0, 0), (0, 0), (0, padded_rows - down_rows))
    ).reshape(count * tok, -1)
    states = (
        ((mid + apply(hidden, w_down)) * valid).astype(jnp.bfloat16).reshape(count, tok, width)
    )

    later, _ = lax.optimization_barrier((prompts, qkv))
    everyone = lax.all_gather(later, "req", axis=0, tiled=True)
    everyone, _ = lax.optimization_barrier((everyone, hidden))
    chosen = jnp.take(perm, initials)
    dealt = jnp.take(everyone, chosen, axis=0).reshape(count * tok, width)
    slot_len = jnp.take(lengths, chosen)
    keep = (places[None, :] < slot_len[:, None]).astype(jnp.bfloat16).reshape(count * tok, 1)
    normed_d = rms_scale(dealt, norm_attn).astype(jnp.bfloat16)
    qkv_d = apply(normed_d, w_qkv) + qkv_bias
    keys_d = rotate(qkv_d[:, width : 2 * width], positions).astype(jnp.bfloat16)
    values_d = qkv_d[:, 2 * width :].astype(jnp.bfloat16)
    key_cache = (keys_d * keep).reshape(count, tok, width)
    value_cache = (values_d * keep).reshape(count, tok, width)
    return (states, key_cache, value_cache)


def solution(mesh):
    placed = (
        P("req", "seq", None),
        P(),
        P(),
        P(),
        P(),
        P("seq", "req"),
        P(),
        P("seq", "req"),
        P("seq", "req"),
        P("seq", "req"),
    )
    return jax.shard_map(
        local,
        mesh=mesh,
        in_specs=placed,
        out_specs=(P("req", "seq", None), P("req", "seq", None), P("req", "seq", None)),
        check_vma=False,
    )
```

```python
import jax
import jax.numpy as jnp
from jax import lax
from jax.sharding import PartitionSpec as P

HEADS = 16
HD = 64


def rms_scale(rows, gain):
    rows = rows.astype(jnp.float32)
    return rows * lax.rsqrt(jnp.mean(rows * rows, axis=-1, keepdims=True) + 1e-06) * gain


def rotate(block, positions):
    half = HD // 2
    count = block.shape[0]
    freqs = jnp.power(1000000.0, -2.0 * jnp.arange(half).astype(jnp.float32) / HD)
    angle = positions[:, None] * freqs[None, :]
    cosine = jnp.cos(angle)[:, None, :]
    sine = jnp.sin(angle)[:, None, :]
    heads = block.reshape(count, -1, HD)
    first = heads[:, :, :half]
    second = heads[:, :, half:]
    turned = jnp.concatenate(
        [first * cosine - second * sine, second * cosine + first * sine], axis=-1
    )
    return turned.reshape(count, -1)


def apply_blocks(inputs, gathered):
    return [jnp.dot(inputs, gathered[r], preferred_element_type=jnp.float32) for r in range(gathered.shape[0])]


def apply(inputs, gathered):
    return jnp.concatenate(apply_blocks(inputs, gathered), axis=1)


def attend_xla(items):
    query, keys, values = items
    length = query.shape[2]
    block = min(512, length)
    scale = HD ** (-0.5)
    pieces = []
    for start in range(0, length, block):
        q_block = query[:, :, start : start + block]
        scores = (
            jnp.einsum("bnid,bnjd->bnij", q_block, keys, preferred_element_type=jnp.float32) * scale
        )
        causal = jnp.arange(length)[None, :] <= (start + jnp.arange(block))[:, None]
        scores = jnp.where(causal[None, None], scores, -1e30)
        top = jnp.max(scores, axis=-1, keepdims=True)
        expo = jnp.exp(scores - top)
        probs = (expo / jnp.sum(expo, axis=-1, keepdims=True)).astype(jnp.bfloat16)
        out = jnp.einsum("bnij,bnjd->bnid", probs, values, preferred_element_type=jnp.float32)
        pieces.append(out.astype(jnp.bfloat16))
    return jnp.concatenate(pieces, axis=2)


def gather_weights(piece, rows=None):
    piece = piece.astype(jnp.bfloat16)
    if rows is not None and rows != piece.shape[0]:
        piece = jnp.pad(piece, ((0, rows - piece.shape[0]), (0, 0)))
    whole = lax.all_gather(piece[None], ("req", "seq"), axis=0, tiled=True)
    return whole.reshape(lax.axis_size("req"), -1, piece.shape[1])


def local(
    prompts,
    perm,
    lengths,
    norm_attn,
    norm_mlp,
    qkv_train,
    qkv_bias,
    out_train,
    gateup_train,
    down_train,
):
    count = prompts.shape[0]
    tok = prompts.shape[1]
    width = prompts.shape[2]
    groups = lax.axis_size("seq")

    blocks = lax.axis_size("req")
    w_qkv = gather_weights(qkv_train)
    w_gu = gather_weights(gateup_train)
    down_rows = down_train.shape[0]
    padded_rows = -(-down_rows // 16) * 16
    down_piece = jnp.pad(down_train.astype(jnp.bfloat16), ((0, padded_rows - down_rows), (0, 0)))
    stacked = jnp.concatenate([down_piece, out_train.astype(jnp.bfloat16)], axis=0)
    rest = lax.all_gather(stacked[None], ("req", "seq"), axis=0, tiled=True)
    rest = rest.reshape(blocks, groups, stacked.shape[0], stacked.shape[1])
    w_down = rest[:, :, :padded_rows].reshape(blocks, -1, down_train.shape[1])
    w_out = rest[:, :, padded_rows:].reshape(blocks, -1, out_train.shape[1])

    places = lax.axis_index("seq") * tok + jnp.arange(tok, dtype=jnp.int32)
    positions = jnp.tile(places, count).astype(jnp.float32)

    initials = lax.axis_index("req") * count + jnp.arange(count, dtype=jnp.int32)
    own_len = jnp.take(lengths, initials)
    valid = (places[None, :] < own_len[:, None]).astype(jnp.float32).reshape(count * tok, 1)
    rows = prompts.reshape(count * tok, width)
    normed = rms_scale(rows, norm_attn).astype(jnp.bfloat16)
    qkv = apply(normed, w_qkv) + qkv_bias
    query = rotate(qkv[:, :width], positions).astype(jnp.bfloat16)
    keys = rotate(qkv[:, width : 2 * width], positions).astype(jnp.bfloat16)
    values = qkv[:, 2 * width :].astype(jnp.bfloat16)
    per_device = count * HEADS // groups

    def to_pairs(array):
        paired = array.reshape(count, tok, HEADS, HD).transpose(0, 2, 1, 3)
        return paired.reshape(groups, per_device, tok, HD)

    gathered = attend_xla(
        (
            lax.all_to_all(to_pairs(query), "seq", split_axis=0, concat_axis=2, tiled=True),
            lax.all_to_all(to_pairs(keys), "seq", split_axis=0, concat_axis=2, tiled=True),
            lax.all_to_all(to_pairs(values), "seq", split_axis=0, concat_axis=2, tiled=True),
        )
    )
    returned = lax.all_to_all(gathered, "seq", split_axis=2, concat_axis=0, tiled=True)
    attended = (
        returned.reshape(count, HEADS, tok, HD).transpose(0, 2, 1, 3).reshape(count * tok, width)
    )
    mid = rows.astype(jnp.float32) + apply(attended, w_out)
    later, mid = lax.optimization_barrier((prompts, mid))
    everyone = lax.all_gather(later, "req", axis=0, tiled=True)
    normed2 = rms_scale(mid, norm_mlp).astype(jnp.bfloat16)
    both = apply_blocks(normed2, w_gu)
    half = len(both) // 2
    hidden = jnp.concatenate(
        [(jax.nn.silu(both[r]) * both[half + r]).astype(jnp.bfloat16) for r in range(half)], axis=1
    )
    hidden = jnp.pad(
        hidden.reshape(count * tok, groups, down_rows), ((0, 0), (0, 0), (0, padded_rows - down_rows))
    ).reshape(count * tok, -1)
    states = (
        ((mid + apply(hidden, w_down)) * valid).astype(jnp.bfloat16).reshape(count, tok, width)
    )

    everyone, _ = lax.optimization_barrier((everyone, hidden))
    chosen = jnp.take(perm, initials)
    dealt = jnp.take(everyone, chosen, axis=0).reshape(count * tok, width)
    slot_len = jnp.take(lengths, chosen)
    keep = (places[None, :] < slot_len[:, None]).astype(jnp.bfloat16).reshape(count * tok, 1)
    normed_d = rms_scale(dealt, norm_attn).astype(jnp.bfloat16)
    qkv_d = apply(normed_d, w_qkv) + qkv_bias
    keys_d = rotate(qkv_d[:, width : 2 * width], positions).astype(jnp.bfloat16)
    values_d = qkv_d[:, 2 * width :].astype(jnp.bfloat16)
    key_cache = (keys_d * keep).reshape(count, tok, width)
    value_cache = (values_d * keep).reshape(count, tok, width)
    return (states, key_cache, value_cache)


def solution(mesh):
    placed = (
        P("req", "seq", None),
        P(),
        P(),
        P(),
        P(),
        P("seq", "req"),
        P(),
        P("seq", "req"),
        P("seq", "req"),
        P("seq", "req"),
    )
    return jax.shard_map(
        local,
        mesh=mesh,
        in_specs=placed,
        out_specs=(P("req", "seq", None), P("req", "seq", None), P("req", "seq", None)),
        check_vma=False,
    )
```

```python
import jax
import jax.numpy as jnp
from jax import lax
from jax.sharding import PartitionSpec as P

HEADS = 16
HD = 64


def rms_scale(rows, gain):
    rows = rows.astype(jnp.float32)
    return rows * lax.rsqrt(jnp.mean(rows * rows, axis=-1, keepdims=True) + 1e-06) * gain


def rotate(block, positions):
    half = HD // 2
    count = block.shape[0]
    freqs = jnp.power(1000000.0, -2.0 * jnp.arange(half).astype(jnp.float32) / HD)
    angle = positions[:, None] * freqs[None, :]
    cosine = jnp.cos(angle)[:, None, :]
    sine = jnp.sin(angle)[:, None, :]
    heads = block.reshape(count, -1, HD)
    first = heads[:, :, :half]
    second = heads[:, :, half:]
    turned = jnp.concatenate(
        [first * cosine - second * sine, second * cosine + first * sine], axis=-1
    )
    return turned.reshape(count, -1)


def apply_blocks(inputs, gathered):
    return [jnp.dot(inputs, gathered[r], preferred_element_type=jnp.float32) for r in range(gathered.shape[0])]


def apply(inputs, gathered):
    return jnp.concatenate(apply_blocks(inputs, gathered), axis=1)


def attend_xla(items):
    query, keys, values = items
    length = query.shape[2]
    block = min(512, length)
    scale = HD ** (-0.5)
    pieces = []
    for start in range(0, length, block):
        reach = start + block
        q_block = query[:, :, start:reach]
        scores = (
            jnp.einsum("bnid,bnjd->bnij", q_block, keys[:, :, :reach], preferred_element_type=jnp.float32)
            * scale
        )
        causal = jnp.arange(reach)[None, :] <= (start + jnp.arange(block))[:, None]
        scores = jnp.where(causal[None, None], scores, -1e30)
        top = jnp.max(scores, axis=-1, keepdims=True)
        expo = jnp.exp(scores - top)
        probs = (expo / jnp.sum(expo, axis=-1, keepdims=True)).astype(jnp.bfloat16)
        out = jnp.einsum("bnij,bnjd->bnid", probs, values[:, :, :reach], preferred_element_type=jnp.float32)
        pieces.append(out.astype(jnp.bfloat16))
    return jnp.concatenate(pieces, axis=2)


def gather_weights(piece, rows=None):
    piece = piece.astype(jnp.bfloat16)
    if rows is not None and rows != piece.shape[0]:
        piece = jnp.pad(piece, ((0, rows - piece.shape[0]), (0, 0)))
    whole = lax.all_gather(piece[None], ("req", "seq"), axis=0, tiled=True)
    return whole.reshape(lax.axis_size("req"), -1, piece.shape[1])


def local(
    prompts,
    perm,
    lengths,
    norm_attn,
    norm_mlp,
    qkv_train,
    qkv_bias,
    out_train,
    gateup_train,
    down_train,
):
    count = prompts.shape[0]
    tok = prompts.shape[1]
    width = prompts.shape[2]
    groups = lax.axis_size("seq")

    blocks = lax.axis_size("req")
    w_qkv = gather_weights(qkv_train)
    w_gu = gather_weights(gateup_train)
    down_rows = down_train.shape[0]
    padded_rows = -(-down_rows // 16) * 16
    down_piece = jnp.pad(down_train.astype(jnp.bfloat16), ((0, padded_rows - down_rows), (0, 0)))
    stacked = jnp.concatenate([down_piece, out_train.astype(jnp.bfloat16)], axis=0)
    rest = lax.all_gather(stacked[None], ("req", "seq"), axis=0, tiled=True)
    rest = rest.reshape(blocks, groups, stacked.shape[0], stacked.shape[1])
    w_down = rest[:, :, :padded_rows].reshape(blocks, -1, down_train.shape[1])
    w_out = rest[:, :, padded_rows:].reshape(blocks, -1, out_train.shape[1])

    places = lax.axis_index("seq") * tok + jnp.arange(tok, dtype=jnp.int32)
    positions = jnp.tile(places, count).astype(jnp.float32)

    initials = lax.axis_index("req") * count + jnp.arange(count, dtype=jnp.int32)
    own_len = jnp.take(lengths, initials)
    valid = (places[None, :] < own_len[:, None]).astype(jnp.float32).reshape(count * tok, 1)
    rows = prompts.reshape(count * tok, width)
    normed = rms_scale(rows, norm_attn).astype(jnp.bfloat16)
    qkv = apply(normed, w_qkv) + qkv_bias
    query = rotate(qkv[:, :width], positions).astype(jnp.bfloat16)
    keys = rotate(qkv[:, width : 2 * width], positions).astype(jnp.bfloat16)
    values = qkv[:, 2 * width :].astype(jnp.bfloat16)
    per_device = count * HEADS // groups

    def to_pairs(array):
        paired = array.reshape(count, tok, HEADS, HD).transpose(0, 2, 1, 3)
        return paired.reshape(groups, per_device, tok, HD)

    gathered = attend_xla(
        (
            lax.all_to_all(to_pairs(query), "seq", split_axis=0, concat_axis=2, tiled=True),
            lax.all_to_all(to_pairs(keys), "seq", split_axis=0, concat_axis=2, tiled=True),
            lax.all_to_all(to_pairs(values), "seq", split_axis=0, concat_axis=2, tiled=True),
        )
    )
    returned = lax.all_to_all(gathered, "seq", split_axis=2, concat_axis=0, tiled=True)
    attended = (
        returned.reshape(count, HEADS, tok, HD).transpose(0, 2, 1, 3).reshape(count * tok, width)
    )
    mid = rows.astype(jnp.float32) + apply(attended, w_out)
    later, mid = lax.optimization_barrier((prompts, mid))
    everyone = lax.all_gather(later, "req", axis=0, tiled=True)
    normed2 = rms_scale(mid, norm_mlp).astype(jnp.bfloat16)
    both = apply_blocks(normed2, w_gu)
    half = len(both) // 2
    hidden = jnp.concatenate(
        [(jax.nn.silu(both[r]) * both[half + r]).astype(jnp.bfloat16) for r in range(half)], axis=1
    )
    hidden = jnp.pad(
        hidden.reshape(count * tok, groups, down_rows), ((0, 0), (0, 0), (0, padded_rows - down_rows))
    ).reshape(count * tok, -1)
    states = (
        ((mid + apply(hidden, w_down)) * valid).astype(jnp.bfloat16).reshape(count, tok, width)
    )

    everyone, _ = lax.optimization_barrier((everyone, hidden))
    chosen = jnp.take(perm, initials)
    dealt = jnp.take(everyone, chosen, axis=0).reshape(count * tok, width)
    slot_len = jnp.take(lengths, chosen)
    keep = (places[None, :] < slot_len[:, None]).astype(jnp.bfloat16).reshape(count * tok, 1)
    normed_d = rms_scale(dealt, norm_attn).astype(jnp.bfloat16)
    skip = width // w_qkv.shape[2]
    kv_d = jnp.concatenate(apply_blocks(normed_d, w_qkv[skip:]), axis=1) + qkv_bias[skip * w_qkv.shape[2] :]
    lead = width - skip * w_qkv.shape[2]
    keys_d = rotate(kv_d[:, lead : lead + width], positions).astype(jnp.bfloat16)
    values_d = kv_d[:, lead + width :].astype(jnp.bfloat16)
    key_cache = (keys_d * keep).reshape(count, tok, width)
    value_cache = (values_d * keep).reshape(count, tok, width)
    return (states, key_cache, value_cache)


def solution(mesh):
    placed = (
        P("req", "seq", None),
        P(),
        P(),
        P(),
        P(),
        P("seq", "req"),
        P(),
        P("seq", "req"),
        P("seq", "req"),
        P("seq", "req"),
    )
    return jax.shard_map(
        local,
        mesh=mesh,
        in_specs=placed,
        out_specs=(P("req", "seq", None), P("req", "seq", None), P("req", "seq", None)),
        check_vma=False,
    )
```

```python
import jax
import jax.numpy as jnp
from jax import lax
from jax.sharding import PartitionSpec as P

HEADS = 16
HD = 64


def rms_scale(rows, gain):
    rows = rows.astype(jnp.float32)
    return rows * lax.rsqrt(jnp.mean(rows * rows, axis=-1, keepdims=True) + 1e-06) * gain


def rotate(block, positions):
    half = HD // 2
    count = block.shape[0]
    freqs = jnp.power(1000000.0, -2.0 * jnp.arange(half).astype(jnp.float32) / HD)
    angle = positions[:, None] * freqs[None, :]
    cosine = jnp.cos(angle)[:, None, :]
    sine = jnp.sin(angle)[:, None, :]
    heads = block.reshape(count, -1, HD)
    first = heads[:, :, :half]
    second = heads[:, :, half:]
    turned = jnp.concatenate(
        [first * cosine - second * sine, second * cosine + first * sine], axis=-1
    )
    return turned.reshape(count, -1)


def apply_blocks(inputs, gathered):
    return [jnp.dot(inputs, gathered[r], preferred_element_type=jnp.float32) for r in range(gathered.shape[0])]


def apply(inputs, gathered):
    return jnp.concatenate(apply_blocks(inputs, gathered), axis=1)


def attend_xla(items):
    query, keys, values = items
    length = query.shape[2]
    block = min(512, length)
    scale = HD ** (-0.5)
    pieces = []
    for start in range(0, length, block):
        reach = start + block
        q_block = query[:, :, start:reach]
        scores = (
            jnp.einsum("bnid,bnjd->bnij", q_block, keys[:, :, :reach], preferred_element_type=jnp.float32)
            * scale
        )
        causal = jnp.arange(reach)[None, :] <= (start + jnp.arange(block))[:, None]
        scores = jnp.where(causal[None, None], scores, -1e30)
        top = jnp.max(scores, axis=-1, keepdims=True)
        expo = jnp.exp(scores - top)
        probs = (expo / jnp.sum(expo, axis=-1, keepdims=True)).astype(jnp.bfloat16)
        out = jnp.einsum("bnij,bnjd->bnid", probs, values[:, :, :reach], preferred_element_type=jnp.float32)
        pieces.append(out.astype(jnp.bfloat16))
    return jnp.concatenate(pieces, axis=2)


def gather_weights(piece, rows=None):
    piece = piece.astype(jnp.bfloat16)
    if rows is not None and rows != piece.shape[0]:
        piece = jnp.pad(piece, ((0, rows - piece.shape[0]), (0, 0)))
    whole = lax.all_gather(piece[None], ("req", "seq"), axis=0, tiled=True)
    return whole.reshape(lax.axis_size("req"), -1, piece.shape[1])


def local(
    prompts,
    perm,
    lengths,
    norm_attn,
    norm_mlp,
    qkv_train,
    qkv_bias,
    out_train,
    gateup_train,
    down_train,
):
    count = prompts.shape[0]
    tok = prompts.shape[1]
    width = prompts.shape[2]
    groups = lax.axis_size("seq")

    blocks = lax.axis_size("req")
    w_qkv = gather_weights(qkv_train)
    prompts_after, w_qkv = lax.optimization_barrier((prompts, w_qkv))
    everyone = lax.all_gather(prompts_after, "req", axis=1, tiled=True)
    everyone = everyone.reshape(prompts.shape[0], -1, prompts.shape[1], prompts.shape[2])

    places = lax.axis_index("seq") * tok + jnp.arange(tok, dtype=jnp.int32)
    positions = jnp.tile(places, count).astype(jnp.float32)

    initials = lax.axis_index("req") * count + jnp.arange(count, dtype=jnp.int32)
    own_len = jnp.take(lengths, initials)
    valid = (places[None, :] < own_len[:, None]).astype(jnp.float32).reshape(count * tok, 1)
    rows = prompts.reshape(count * tok, width)
    normed = rms_scale(rows, norm_attn).astype(jnp.bfloat16)
    qkv = apply(normed, w_qkv) + qkv_bias
    gateup_after, down_after, out_after, qkv = lax.optimization_barrier((gateup_train, down_train, out_train, qkv))
    w_gu = gather_weights(gateup_after)
    down_rows = down_train.shape[0]
    padded_rows = -(-down_rows // 16) * 16
    down_piece = jnp.pad(down_after.astype(jnp.bfloat16), ((0, padded_rows - down_rows), (0, 0)))
    stacked = jnp.concatenate([down_piece, out_after.astype(jnp.bfloat16)], axis=0)
    rest = lax.all_gather(stacked[None], ("req", "seq"), axis=0, tiled=True)
    rest = rest.reshape(blocks, groups, stacked.shape[0], stacked.shape[1])
    w_down = rest[:, :, :padded_rows].reshape(blocks, -1, down_train.shape[1])
    w_out = rest[:, :, padded_rows:].reshape(blocks, -1, out_train.shape[1])

    query = rotate(qkv[:, :width], positions).astype(jnp.bfloat16)
    keys = rotate(qkv[:, width : 2 * width], positions).astype(jnp.bfloat16)
    values = qkv[:, 2 * width :].astype(jnp.bfloat16)
    per_device = count * HEADS // groups

    def to_pairs(array):
        paired = array.reshape(count, tok, HEADS, HD).transpose(0, 2, 1, 3)
        return paired.reshape(groups, per_device, tok, HD)

    gathered = attend_xla(
        (
            lax.all_to_all(to_pairs(query), "seq", split_axis=0, concat_axis=2, tiled=True),
            lax.all_to_all(to_pairs(keys), "seq", split_axis=0, concat_axis=2, tiled=True),
            lax.all_to_all(to_pairs(values), "seq", split_axis=0, concat_axis=2, tiled=True),
        )
    )
    returned = lax.all_to_all(gathered, "seq", split_axis=2, concat_axis=0, tiled=True)
    attended = (
        returned.reshape(count, HEADS, tok, HD).transpose(0, 2, 1, 3).reshape(count * tok, width)
    )
    mid = rows.astype(jnp.float32) + apply(attended, w_out)
    normed2 = rms_scale(mid, norm_mlp).astype(jnp.bfloat16)
    both = apply_blocks(normed2, w_gu)
    half = len(both) // 2
    hidden = jnp.concatenate(
        [(jax.nn.silu(both[r]) * both[half + r]).astype(jnp.bfloat16) for r in range(half)], axis=1
    )
    hidden = jnp.pad(
        hidden.reshape(count * tok, groups, down_rows), ((0, 0), (0, 0), (0, padded_rows - down_rows))
    ).reshape(count * tok, -1)
    states = (
        ((mid + apply(hidden, w_down)) * valid).astype(jnp.bfloat16).reshape(count, tok, width)
    )

    chosen = jnp.take(perm, initials)
    dealt = everyone[chosen % count, chosen // count].reshape(count * tok, width)
    slot_len = jnp.take(lengths, chosen)
    keep = (places[None, :] < slot_len[:, None]).astype(jnp.bfloat16).reshape(count * tok, 1)
    normed_d = rms_scale(dealt, norm_attn).astype(jnp.bfloat16)
    skip = width // w_qkv.shape[2]
    kv_d = jnp.concatenate(apply_blocks(normed_d, w_qkv[skip:]), axis=1) + qkv_bias[skip * w_qkv.shape[2] :]
    lead = width - skip * w_qkv.shape[2]
    keys_d = rotate(kv_d[:, lead : lead + width], positions).astype(jnp.bfloat16)
    values_d = kv_d[:, lead + width :].astype(jnp.bfloat16)
    key_cache = (keys_d * keep).reshape(count, tok, width)
    value_cache = (values_d * keep).reshape(count, tok, width)
    return (states, key_cache, value_cache)


def solution(mesh):
    placed = (
        P("req", "seq", None),
        P(),
        P(),
        P(),
        P(),
        P("seq", "req"),
        P(),
        P("seq", "req"),
        P("seq", "req"),
        P("seq", "req"),
    )
    return jax.shard_map(
        local,
        mesh=mesh,
        in_specs=placed,
        out_specs=(P("req", "seq", None), P("req", "seq", None), P("req", "seq", None)),
        check_vma=False,
    )
```

```python
import jax
import jax.numpy as jnp
from jax import lax
from jax.sharding import PartitionSpec as P

HEADS = 16
HD = 64


def rms_scale(rows, gain):
    rows = rows.astype(jnp.float32)
    return rows * lax.rsqrt(jnp.mean(rows * rows, axis=-1, keepdims=True) + 1e-06) * gain


def rotate(block, positions):
    half = HD // 2
    count = block.shape[0]
    freqs = jnp.power(1000000.0, -2.0 * jnp.arange(half).astype(jnp.float32) / HD)
    angle = positions[:, None] * freqs[None, :]
    cosine = jnp.cos(angle)[:, None, :]
    sine = jnp.sin(angle)[:, None, :]
    heads = block.reshape(count, -1, HD)
    first = heads[:, :, :half]
    second = heads[:, :, half:]
    turned = jnp.concatenate(
        [first * cosine - second * sine, second * cosine + first * sine], axis=-1
    )
    return turned.reshape(count, -1)


def apply_blocks(inputs, gathered):
    return [jnp.dot(inputs, gathered[r], preferred_element_type=jnp.float32) for r in range(gathered.shape[0])]


def apply(inputs, gathered):
    return jnp.concatenate(apply_blocks(inputs, gathered), axis=1)


def attend_xla(items):
    query, keys, values = items
    length = query.shape[2]
    block = min(512, length)
    scale = HD ** (-0.5)
    pieces = []
    for start in range(0, length, block):
        reach = start + block
        q_block = query[:, :, start:reach]
        scores = (
            jnp.einsum("bnid,bnjd->bnij", q_block, keys[:, :, :reach], preferred_element_type=jnp.float32)
            * scale
        )
        causal = jnp.arange(reach)[None, :] <= (start + jnp.arange(block))[:, None]
        scores = jnp.where(causal[None, None], scores, -1e30)
        top = jnp.max(scores, axis=-1, keepdims=True)
        expo = jnp.exp(scores - top)
        probs = (expo / jnp.sum(expo, axis=-1, keepdims=True)).astype(jnp.bfloat16)
        out = jnp.einsum("bnij,bnjd->bnid", probs, values[:, :, :reach], preferred_element_type=jnp.float32)
        pieces.append(out.astype(jnp.bfloat16))
    return jnp.concatenate(pieces, axis=2)


def gather_weights(piece, rows=None):
    piece = piece.astype(jnp.bfloat16)
    if rows is not None and rows != piece.shape[0]:
        piece = jnp.pad(piece, ((0, rows - piece.shape[0]), (0, 0)))
    whole = lax.all_gather(piece[None], ("req", "seq"), axis=0, tiled=True)
    return whole.reshape(lax.axis_size("req"), -1, piece.shape[1])


def local(
    prompts,
    perm,
    lengths,
    norm_attn,
    norm_mlp,
    qkv_train,
    qkv_bias,
    out_train,
    gateup_train,
    down_train,
):
    count = prompts.shape[0]
    tok = prompts.shape[1]
    width = prompts.shape[2]
    groups = lax.axis_size("seq")

    blocks = lax.axis_size("req")
    w_qkv = gather_weights(qkv_train)
    w_gu = gather_weights(gateup_train)
    down_rows = down_train.shape[0]
    padded_rows = -(-down_rows // 16) * 16
    down_piece = jnp.pad(down_train.astype(jnp.bfloat16), ((0, padded_rows - down_rows), (0, 0)))
    stacked = jnp.concatenate([down_piece, out_train.astype(jnp.bfloat16)], axis=0)
    rest = lax.all_gather(stacked[None], ("req", "seq"), axis=0, tiled=True)
    rest = rest.reshape(blocks, groups, stacked.shape[0], stacked.shape[1])
    w_down = rest[:, :, :padded_rows].reshape(blocks, -1, down_train.shape[1])
    w_out = rest[:, :, padded_rows:].reshape(blocks, -1, out_train.shape[1])

    places = lax.axis_index("seq") * tok + jnp.arange(tok, dtype=jnp.int32)
    positions = jnp.tile(places, count).astype(jnp.float32)

    initials = lax.axis_index("req") * count + jnp.arange(count, dtype=jnp.int32)
    own_len = jnp.take(lengths, initials)
    valid = (places[None, :] < own_len[:, None]).astype(jnp.float32).reshape(count * tok, 1)
    rows = prompts.reshape(count * tok, width)
    normed = rms_scale(rows, norm_attn).astype(jnp.bfloat16)
    qkv = apply(normed, w_qkv) + qkv_bias
    query = rotate(qkv[:, :width], positions).astype(jnp.bfloat16)
    keys = rotate(qkv[:, width : 2 * width], positions).astype(jnp.bfloat16)
    values = qkv[:, 2 * width :].astype(jnp.bfloat16)
    per_device = count * HEADS // groups

    def to_pairs(array):
        paired = array.reshape(count, tok, HEADS, HD).transpose(0, 2, 1, 3)
        return paired.reshape(groups, per_device, tok, HD)

    gathered = attend_xla(
        (
            lax.all_to_all(to_pairs(query), "seq", split_axis=0, concat_axis=2, tiled=True),
            lax.all_to_all(to_pairs(keys), "seq", split_axis=0, concat_axis=2, tiled=True),
            lax.all_to_all(to_pairs(values), "seq", split_axis=0, concat_axis=2, tiled=True),
        )
    )
    returned = lax.all_to_all(gathered, "seq", split_axis=2, concat_axis=0, tiled=True)
    attended = (
        returned.reshape(count, HEADS, tok, HD).transpose(0, 2, 1, 3).reshape(count * tok, width)
    )
    mid = rows.astype(jnp.float32) + apply(attended, w_out)
    own_keep = valid.astype(jnp.bfloat16)
    cached = jnp.concatenate([keys * own_keep, values * own_keep], axis=1).reshape(count, tok, 2 * width)
    cached, mid = lax.optimization_barrier((cached, mid))
    everyone = lax.all_gather(cached, "req", axis=0, tiled=True)
    normed2 = rms_scale(mid, norm_mlp).astype(jnp.bfloat16)
    both = apply_blocks(normed2, w_gu)
    half = len(both) // 2
    hidden = jnp.concatenate(
        [(jax.nn.silu(both[r]) * both[half + r]).astype(jnp.bfloat16) for r in range(half)], axis=1
    )
    hidden = jnp.pad(
        hidden.reshape(count * tok, groups, down_rows), ((0, 0), (0, 0), (0, padded_rows - down_rows))
    ).reshape(count * tok, -1)
    states = (
        ((mid + apply(hidden, w_down)) * valid).astype(jnp.bfloat16).reshape(count, tok, width)
    )

    chosen = jnp.take(perm, initials)
    dealt = jnp.take(everyone, chosen, axis=0)
    key_cache = dealt[:, :, :width]
    value_cache = dealt[:, :, width:]
    return (states, key_cache, value_cache)


def solution(mesh):
    placed = (
        P("req", "seq", None),
        P(),
        P(),
        P(),
        P(),
        P("seq", "req"),
        P(),
        P("seq", "req"),
        P("seq", "req"),
        P("seq", "req"),
    )
    return jax.shard_map(
        local,
        mesh=mesh,
        in_specs=placed,
        out_specs=(P("req", "seq", None), P("req", "seq", None), P("req", "seq", None)),
        check_vma=False,
    )
```

```python
import jax
import jax.numpy as jnp
from jax import lax
from jax.sharding import PartitionSpec as P

HEADS = 16
HD = 64


def rms_scale(rows, gain):
    rows = rows.astype(jnp.float32)
    return rows * lax.rsqrt(jnp.mean(rows * rows, axis=-1, keepdims=True) + 1e-06) * gain


def rotate(block, positions):
    half = HD // 2
    count = block.shape[0]
    freqs = jnp.power(1000000.0, -2.0 * jnp.arange(half).astype(jnp.float32) / HD)
    angle = positions[:, None] * freqs[None, :]
    cosine = jnp.cos(angle)[:, None, :]
    sine = jnp.sin(angle)[:, None, :]
    heads = block.reshape(count, -1, HD)
    first = heads[:, :, :half]
    second = heads[:, :, half:]
    turned = jnp.concatenate(
        [first * cosine - second * sine, second * cosine + first * sine], axis=-1
    )
    return turned.reshape(count, -1)


def apply_blocks(inputs, gathered):
    return [jnp.dot(inputs, gathered[r], preferred_element_type=jnp.float32) for r in range(gathered.shape[0])]


def apply(inputs, gathered):
    return jnp.concatenate(apply_blocks(inputs, gathered), axis=1)


def attend_xla(items):
    query, keys, values = items
    length = query.shape[2]
    block = min(512, length)
    scale = HD ** (-0.5)
    pieces = []
    for start in range(0, length, block):
        reach = start + block
        q_block = query[:, :, start:reach]
        scores = (
            jnp.einsum("bnid,bnjd->bnij", q_block, keys[:, :, :reach], preferred_element_type=jnp.float32)
            * scale
        )
        causal = jnp.arange(reach)[None, :] <= (start + jnp.arange(block))[:, None]
        scores = jnp.where(causal[None, None], scores, -1e30)
        top = jnp.max(scores, axis=-1, keepdims=True)
        expo = jnp.exp(scores - top)
        probs = (expo / jnp.sum(expo, axis=-1, keepdims=True)).astype(jnp.bfloat16)
        out = jnp.einsum("bnij,bnjd->bnid", probs, values[:, :, :reach], preferred_element_type=jnp.float32)
        pieces.append(out.astype(jnp.bfloat16))
    return jnp.concatenate(pieces, axis=2)


def gather_weights(piece, rows=None):
    piece = piece.astype(jnp.bfloat16)
    if rows is not None and rows != piece.shape[0]:
        piece = jnp.pad(piece, ((0, rows - piece.shape[0]), (0, 0)))
    whole = lax.all_gather(piece[None], ("req", "seq"), axis=0, tiled=True)
    return whole.reshape(lax.axis_size("req"), -1, piece.shape[1])


def local(
    prompts,
    perm,
    lengths,
    norm_attn,
    norm_mlp,
    qkv_train,
    qkv_bias,
    out_train,
    gateup_train,
    down_train,
):
    count = prompts.shape[0]
    tok = prompts.shape[1]
    width = prompts.shape[2]
    groups = lax.axis_size("seq")

    blocks = lax.axis_size("req")
    w_qkv = gather_weights(qkv_train)
    w_gu = gather_weights(gateup_train)
    down_rows = down_train.shape[0]
    padded_rows = -(-down_rows // 16) * 16
    down_piece = jnp.pad(down_train.astype(jnp.bfloat16), ((0, padded_rows - down_rows), (0, 0)))
    stacked = jnp.concatenate([down_piece, out_train.astype(jnp.bfloat16)], axis=0)
    rest = lax.all_gather(stacked[None], ("req", "seq"), axis=0, tiled=True)
    rest = rest.reshape(blocks, groups, stacked.shape[0], stacked.shape[1])
    w_down = rest[:, :, :padded_rows].reshape(blocks, -1, down_train.shape[1])
    w_out = rest[:, :, padded_rows:].reshape(blocks, -1, out_train.shape[1])

    places = lax.axis_index("seq") * tok + jnp.arange(tok, dtype=jnp.int32)
    positions = jnp.tile(places, count).astype(jnp.float32)

    initials = lax.axis_index("req") * count + jnp.arange(count, dtype=jnp.int32)
    own_len = jnp.take(lengths, initials)
    valid = (places[None, :] < own_len[:, None]).astype(jnp.float32).reshape(count * tok, 1)
    rows = prompts.reshape(count * tok, width)
    normed = rms_scale(rows, norm_attn).astype(jnp.bfloat16)
    qkv = apply(normed, w_qkv) + qkv_bias
    query = rotate(qkv[:, :width], positions).astype(jnp.bfloat16)
    keys = rotate(qkv[:, width : 2 * width], positions).astype(jnp.bfloat16)
    values = qkv[:, 2 * width :].astype(jnp.bfloat16)
    per_device = count * HEADS // groups

    def to_pairs(array):
        paired = array.reshape(count, tok, HEADS, HD).transpose(0, 2, 1, 3)
        return paired.reshape(groups, per_device, tok, HD)

    gathered = attend_xla(
        (
            lax.all_to_all(to_pairs(query), "seq", split_axis=0, concat_axis=2, tiled=True),
            lax.all_to_all(to_pairs(keys), "seq", split_axis=0, concat_axis=2, tiled=True),
            lax.all_to_all(to_pairs(values), "seq", split_axis=0, concat_axis=2, tiled=True),
        )
    )
    own_keep = valid.astype(jnp.bfloat16)
    cached = jnp.concatenate([keys * own_keep, values * own_keep], axis=1).reshape(count, tok, 2 * width)
    cached, gathered, w_gu = lax.optimization_barrier((cached, gathered, w_gu))
    everyone = lax.all_gather(cached, "req", axis=0, tiled=True)
    returned = lax.all_to_all(gathered, "seq", split_axis=2, concat_axis=0, tiled=True)
    attended = (
        returned.reshape(count, HEADS, tok, HD).transpose(0, 2, 1, 3).reshape(count * tok, width)
    )
    mid = rows.astype(jnp.float32) + apply(attended, w_out)
    normed2 = rms_scale(mid, norm_mlp).astype(jnp.bfloat16)
    both = apply_blocks(normed2, w_gu)
    half = len(both) // 2
    hidden = jnp.concatenate(
        [(jax.nn.silu(both[r]) * both[half + r]).astype(jnp.bfloat16) for r in range(half)], axis=1
    )
    hidden = jnp.pad(
        hidden.reshape(count * tok, groups, down_rows), ((0, 0), (0, 0), (0, padded_rows - down_rows))
    ).reshape(count * tok, -1)
    states = (
        ((mid + apply(hidden, w_down)) * valid).astype(jnp.bfloat16).reshape(count, tok, width)
    )

    chosen = jnp.take(perm, initials)
    dealt = jnp.take(everyone, chosen, axis=0)
    key_cache = dealt[:, :, :width]
    value_cache = dealt[:, :, width:]
    return (states, key_cache, value_cache)


def solution(mesh):
    placed = (
        P("req", "seq", None),
        P(),
        P(),
        P(),
        P(),
        P("seq", "req"),
        P(),
        P("seq", "req"),
        P("seq", "req"),
        P("seq", "req"),
    )
    return jax.shard_map(
        local,
        mesh=mesh,
        in_specs=placed,
        out_specs=(P("req", "seq", None), P("req", "seq", None), P("req", "seq", None)),
        check_vma=False,
    )
```

```python
import jax
import jax.numpy as jnp
from jax import lax
from jax.sharding import PartitionSpec as P

HEADS = 16
HD = 64


def rms_scale(rows, gain):
    rows = rows.astype(jnp.float32)
    return rows * lax.rsqrt(jnp.mean(rows * rows, axis=-1, keepdims=True) + 1e-06) * gain


def rotate(block, positions):
    half = HD // 2
    count = block.shape[0]
    freqs = jnp.power(1000000.0, -2.0 * jnp.arange(half).astype(jnp.float32) / HD)
    angle = positions[:, None] * freqs[None, :]
    cosine = jnp.cos(angle)[:, None, :]
    sine = jnp.sin(angle)[:, None, :]
    heads = block.reshape(count, -1, HD)
    first = heads[:, :, :half]
    second = heads[:, :, half:]
    turned = jnp.concatenate(
        [first * cosine - second * sine, second * cosine + first * sine], axis=-1
    )
    return turned.reshape(count, -1)


def apply_blocks(inputs, gathered):
    return [jnp.dot(inputs, gathered[r], preferred_element_type=jnp.float32) for r in range(gathered.shape[0])]


def apply(inputs, gathered):
    return jnp.concatenate(apply_blocks(inputs, gathered), axis=1)


def attend_xla(items):
    query, keys, values = items
    length = query.shape[2]
    block = min(512, length)
    scale = HD ** (-0.5)
    pieces = []
    for start in range(0, length, block):
        reach = start + block
        q_block = query[:, :, start:reach]
        scores = (
            jnp.einsum("bnid,bnjd->bnij", q_block, keys[:, :, :reach], preferred_element_type=jnp.float32)
            * scale
        )
        causal = jnp.arange(reach)[None, :] <= (start + jnp.arange(block))[:, None]
        scores = jnp.where(causal[None, None], scores, -1e30)
        top = jnp.max(scores, axis=-1, keepdims=True)
        expo = jnp.exp(scores - top)
        probs = (expo / jnp.sum(expo, axis=-1, keepdims=True)).astype(jnp.bfloat16)
        out = jnp.einsum("bnij,bnjd->bnid", probs, values[:, :, :reach], preferred_element_type=jnp.float32)
        pieces.append(out.astype(jnp.bfloat16))
    return jnp.concatenate(pieces, axis=2)


def gather_weights(piece, rows=None):
    piece = piece.astype(jnp.bfloat16)
    if rows is not None and rows != piece.shape[0]:
        piece = jnp.pad(piece, ((0, rows - piece.shape[0]), (0, 0)))
    whole = lax.all_gather(piece[None], ("req", "seq"), axis=0, tiled=True)
    return whole.reshape(lax.axis_size("req"), -1, piece.shape[1])


def local(
    prompts,
    perm,
    lengths,
    norm_attn,
    norm_mlp,
    qkv_train,
    qkv_bias,
    out_train,
    gateup_train,
    down_train,
):
    count = prompts.shape[0]
    tok = prompts.shape[1]
    width = prompts.shape[2]
    groups = lax.axis_size("seq")

    blocks = lax.axis_size("req")
    qkv_piece = qkv_train.astype(jnp.bfloat16)[None]
    devices = blocks * groups
    w_qkv = lax.all_to_all(
        jnp.broadcast_to(qkv_piece, (devices,) + qkv_piece.shape[1:]), ("req", "seq"), 0, 0, tiled=True
    ).reshape(blocks, -1, qkv_train.shape[1])
    w_gu = gather_weights(gateup_train)
    down_rows = down_train.shape[0]
    padded_rows = -(-down_rows // 16) * 16
    down_piece = jnp.pad(down_train.astype(jnp.bfloat16), ((0, padded_rows - down_rows), (0, 0)))
    stacked = jnp.concatenate([down_piece, out_train.astype(jnp.bfloat16)], axis=0)
    rest = lax.all_gather(stacked[None], ("req", "seq"), axis=0, tiled=True)
    rest = rest.reshape(blocks, groups, stacked.shape[0], stacked.shape[1])
    w_down = rest[:, :, :padded_rows].reshape(blocks, -1, down_train.shape[1])
    w_out = rest[:, :, padded_rows:].reshape(blocks, -1, out_train.shape[1])

    places = lax.axis_index("seq") * tok + jnp.arange(tok, dtype=jnp.int32)
    positions = jnp.tile(places, count).astype(jnp.float32)

    initials = lax.axis_index("req") * count + jnp.arange(count, dtype=jnp.int32)
    own_len = jnp.take(lengths, initials)
    valid = (places[None, :] < own_len[:, None]).astype(jnp.float32).reshape(count * tok, 1)
    rows = prompts.reshape(count * tok, width)
    normed = rms_scale(rows, norm_attn).astype(jnp.bfloat16)
    qkv = apply(normed, w_qkv) + qkv_bias
    query = rotate(qkv[:, :width], positions).astype(jnp.bfloat16)
    keys = rotate(qkv[:, width : 2 * width], positions).astype(jnp.bfloat16)
    values = qkv[:, 2 * width :].astype(jnp.bfloat16)
    per_device = count * HEADS // groups

    def to_pairs(array):
        paired = array.reshape(count, tok, HEADS, HD).transpose(0, 2, 1, 3)
        return paired.reshape(groups, per_device, tok, HD)

    gathered = attend_xla(
        (
            lax.all_to_all(to_pairs(query), "seq", split_axis=0, concat_axis=2, tiled=True),
            lax.all_to_all(to_pairs(keys), "seq", split_axis=0, concat_axis=2, tiled=True),
            lax.all_to_all(to_pairs(values), "seq", split_axis=0, concat_axis=2, tiled=True),
        )
    )
    own_keep = valid.astype(jnp.bfloat16)
    cached = jnp.concatenate([keys * own_keep, values * own_keep], axis=1).reshape(count, tok, 2 * width)
    cached, gathered, w_gu = lax.optimization_barrier((cached, gathered, w_gu))
    everyone = lax.all_gather(cached, "req", axis=0, tiled=True)
    returned = lax.all_to_all(gathered, "seq", split_axis=2, concat_axis=0, tiled=True)
    attended = (
        returned.reshape(count, HEADS, tok, HD).transpose(0, 2, 1, 3).reshape(count * tok, width)
    )
    mid = rows.astype(jnp.float32) + apply(attended, w_out)
    normed2 = rms_scale(mid, norm_mlp).astype(jnp.bfloat16)
    both = apply_blocks(normed2, w_gu)
    half = len(both) // 2
    hidden = jnp.concatenate(
        [(jax.nn.silu(both[r]) * both[half + r]).astype(jnp.bfloat16) for r in range(half)], axis=1
    )
    hidden = jnp.pad(
        hidden.reshape(count * tok, groups, down_rows), ((0, 0), (0, 0), (0, padded_rows - down_rows))
    ).reshape(count * tok, -1)
    states = (
        ((mid + apply(hidden, w_down)) * valid).astype(jnp.bfloat16).reshape(count, tok, width)
    )

    chosen = jnp.take(perm, initials)
    dealt = jnp.take(everyone, chosen, axis=0)
    key_cache = dealt[:, :, :width]
    value_cache = dealt[:, :, width:]
    return (states, key_cache, value_cache)


def solution(mesh):
    placed = (
        P("req", "seq", None),
        P(),
        P(),
        P(),
        P(),
        P("seq", "req"),
        P(),
        P("seq", "req"),
        P("seq", "req"),
        P("seq", "req"),
    )
    return jax.shard_map(
        local,
        mesh=mesh,
        in_specs=placed,
        out_specs=(P("req", "seq", None), P("req", "seq", None), P("req", "seq", None)),
        check_vma=False,
    )
```

```python
import jax
import jax.numpy as jnp
from jax import lax
from jax.sharding import PartitionSpec as P

HEADS = 16
HD = 64


def rms_scale(rows, gain):
    rows = rows.astype(jnp.float32)
    return rows * lax.rsqrt(jnp.mean(rows * rows, axis=-1, keepdims=True) + 1e-06) * gain


def rotate(block, positions):
    half = HD // 2
    count = block.shape[0]
    freqs = jnp.power(1000000.0, -2.0 * jnp.arange(half).astype(jnp.float32) / HD)
    angle = positions[:, None] * freqs[None, :]
    cosine = jnp.cos(angle)[:, None, :]
    sine = jnp.sin(angle)[:, None, :]
    heads = block.reshape(count, -1, HD)
    first = heads[:, :, :half]
    second = heads[:, :, half:]
    turned = jnp.concatenate(
        [first * cosine - second * sine, second * cosine + first * sine], axis=-1
    )
    return turned.reshape(count, -1)


def apply_blocks(inputs, gathered):
    return [jnp.dot(inputs, gathered[r], preferred_element_type=jnp.float32) for r in range(gathered.shape[0])]


def apply(inputs, gathered):
    return jnp.concatenate(apply_blocks(inputs, gathered), axis=1)


def attend_xla(items):
    query, keys, values = items
    length = query.shape[2]
    block = min(512, length)
    scale = HD ** (-0.5)
    pieces = []
    for start in range(0, length, block):
        reach = start + block
        q_block = query[:, :, start:reach]
        scores = (
            jnp.einsum("bnid,bnjd->bnij", q_block, keys[:, :, :reach], preferred_element_type=jnp.float32)
            * scale
        )
        causal = jnp.arange(reach)[None, :] <= (start + jnp.arange(block))[:, None]
        scores = jnp.where(causal[None, None], scores, -1e30)
        top = jnp.max(scores, axis=-1, keepdims=True)
        expo = jnp.exp(scores - top)
        probs = (expo / jnp.sum(expo, axis=-1, keepdims=True)).astype(jnp.bfloat16)
        out = jnp.einsum("bnij,bnjd->bnid", probs, values[:, :, :reach], preferred_element_type=jnp.float32)
        pieces.append(out.astype(jnp.bfloat16))
    return jnp.concatenate(pieces, axis=2)


def gather_weights(piece, rows=None):
    piece = piece.astype(jnp.bfloat16)
    if rows is not None and rows != piece.shape[0]:
        piece = jnp.pad(piece, ((0, rows - piece.shape[0]), (0, 0)))
    whole = lax.all_gather(piece[None], ("req", "seq"), axis=0, tiled=True)
    return whole.reshape(lax.axis_size("req"), -1, piece.shape[1])


def local(
    prompts,
    perm,
    lengths,
    norm_attn,
    norm_mlp,
    qkv_train,
    qkv_bias,
    out_train,
    gateup_train,
    down_train,
):
    count = prompts.shape[0]
    tok = prompts.shape[1]
    width = prompts.shape[2]
    groups = lax.axis_size("seq")

    blocks = lax.axis_size("req")
    w_qkv = gather_weights(qkv_train)
    w_gu = gather_weights(gateup_train)
    down_rows = down_train.shape[0]
    padded_rows = -(-down_rows // 16) * 16
    down_piece = jnp.pad(down_train.astype(jnp.bfloat16), ((0, padded_rows - down_rows), (0, 0)))
    stacked = jnp.concatenate([down_piece, out_train.astype(jnp.bfloat16)], axis=0)
    rest = lax.all_gather(stacked[None], ("req", "seq"), axis=0, tiled=True)
    rest = rest.reshape(blocks, groups, stacked.shape[0], stacked.shape[1])
    w_down = rest[:, :, :padded_rows].reshape(blocks, -1, down_train.shape[1])
    w_out = rest[:, :, padded_rows:].reshape(blocks, -1, out_train.shape[1])

    places = lax.axis_index("seq") * tok + jnp.arange(tok, dtype=jnp.int32)
    positions = jnp.tile(places, count).astype(jnp.float32)

    initials = lax.axis_index("req") * count + jnp.arange(count, dtype=jnp.int32)
    own_len = jnp.take(lengths, initials)
    valid = (places[None, :] < own_len[:, None]).astype(jnp.float32).reshape(count * tok, 1)
    rows = prompts.reshape(count * tok, width)
    normed = rms_scale(rows, norm_attn).astype(jnp.bfloat16)
    qkv = apply(normed, w_qkv) + qkv_bias
    query = rotate(qkv[:, :width], positions).astype(jnp.bfloat16)
    keys = rotate(qkv[:, width : 2 * width], positions).astype(jnp.bfloat16)
    values = qkv[:, 2 * width :].astype(jnp.bfloat16)
    per_device = count * HEADS // groups

    def to_pairs(array):
        paired = array.reshape(count, tok, HEADS, HD).transpose(0, 2, 1, 3)
        return paired.reshape(groups, per_device, tok, HD)

    gathered = attend_xla(
        (
            lax.all_to_all(to_pairs(query), "seq", split_axis=0, concat_axis=2, tiled=True),
            lax.all_to_all(to_pairs(keys), "seq", split_axis=0, concat_axis=2, tiled=True),
            lax.all_to_all(to_pairs(values), "seq", split_axis=0, concat_axis=2, tiled=True),
        )
    )
    returned = lax.all_to_all(gathered, "seq", split_axis=2, concat_axis=0, tiled=True)
    own_keep = valid.astype(jnp.bfloat16)
    cached = jnp.concatenate([keys * own_keep, values * own_keep], axis=1).reshape(count, tok, 2 * width)
    cached, returned, w_gu = lax.optimization_barrier((cached, returned, w_gu))
    everyone = lax.all_gather(cached, "req", axis=0, tiled=True)
    attended = (
        returned.reshape(count, HEADS, tok, HD).transpose(0, 2, 1, 3).reshape(count * tok, width)
    )
    mid = rows.astype(jnp.float32) + apply(attended, w_out)
    normed2 = rms_scale(mid, norm_mlp).astype(jnp.bfloat16)
    both = apply_blocks(normed2, w_gu)
    half = len(both) // 2
    hidden = jnp.concatenate(
        [(jax.nn.silu(both[r]) * both[half + r]).astype(jnp.bfloat16) for r in range(half)], axis=1
    )
    hidden = jnp.pad(
        hidden.reshape(count * tok, groups, down_rows), ((0, 0), (0, 0), (0, padded_rows - down_rows))
    ).reshape(count * tok, -1)
    states = (
        ((mid + apply(hidden, w_down)) * valid).astype(jnp.bfloat16).reshape(count, tok, width)
    )

    chosen = jnp.take(perm, initials)
    dealt = jnp.take(everyone, chosen, axis=0)
    key_cache = dealt[:, :, :width]
    value_cache = dealt[:, :, width:]
    return (states, key_cache, value_cache)


def solution(mesh):
    placed = (
        P("req", "seq", None),
        P(),
        P(),
        P(),
        P(),
        P("seq", "req"),
        P(),
        P("seq", "req"),
        P("seq", "req"),
        P("seq", "req"),
    )
    return jax.shard_map(
        local,
        mesh=mesh,
        in_specs=placed,
        out_specs=(P("req", "seq", None), P("req", "seq", None), P("req", "seq", None)),
        check_vma=False,
    )
```

```python
import jax
import jax.numpy as jnp
from jax import lax
from jax.sharding import PartitionSpec as P

HEADS = 16
HD = 64


def rms_scale(rows, gain):
    rows = rows.astype(jnp.float32)
    return rows * lax.rsqrt(jnp.mean(rows * rows, axis=-1, keepdims=True) + 1e-06) * gain


def rotate(block, positions):
    half = HD // 2
    count = block.shape[0]
    freqs = jnp.power(1000000.0, -2.0 * jnp.arange(half).astype(jnp.float32) / HD)
    angle = positions[:, None] * freqs[None, :]
    cosine = jnp.cos(angle)[:, None, :]
    sine = jnp.sin(angle)[:, None, :]
    heads = block.reshape(count, -1, HD)
    first = heads[:, :, :half]
    second = heads[:, :, half:]
    turned = jnp.concatenate(
        [first * cosine - second * sine, second * cosine + first * sine], axis=-1
    )
    return turned.reshape(count, -1)


def apply_blocks(inputs, gathered):
    return [jnp.dot(inputs, gathered[r], preferred_element_type=jnp.float32) for r in range(gathered.shape[0])]


def apply(inputs, gathered):
    return jnp.concatenate(apply_blocks(inputs, gathered), axis=1)


def attend_xla(items):
    query, keys, values = items
    length = query.shape[2]
    block = min(256, length)
    scale = HD ** (-0.5)
    pieces = []
    for start in range(0, length, block):
        reach = start + block
        q_block = query[:, :, start:reach]
        scores = (
            jnp.einsum("bnid,bnjd->bnij", q_block, keys[:, :, :reach], preferred_element_type=jnp.float32)
            * scale
        )
        causal = jnp.arange(reach)[None, :] <= (start + jnp.arange(block))[:, None]
        scores = jnp.where(causal[None, None], scores, -1e30)
        top = jnp.max(scores, axis=-1, keepdims=True)
        expo = jnp.exp(scores - top)
        probs = (expo / jnp.sum(expo, axis=-1, keepdims=True)).astype(jnp.bfloat16)
        out = jnp.einsum("bnij,bnjd->bnid", probs, values[:, :, :reach], preferred_element_type=jnp.float32)
        pieces.append(out.astype(jnp.bfloat16))
    return jnp.concatenate(pieces, axis=2)


def gather_weights(piece, rows=None):
    piece = piece.astype(jnp.bfloat16)
    if rows is not None and rows != piece.shape[0]:
        piece = jnp.pad(piece, ((0, rows - piece.shape[0]), (0, 0)))
    whole = lax.all_gather(piece[None], ("req", "seq"), axis=0, tiled=True)
    return whole.reshape(lax.axis_size("req"), -1, piece.shape[1])


def local(
    prompts,
    perm,
    lengths,
    norm_attn,
    norm_mlp,
    qkv_train,
    qkv_bias,
    out_train,
    gateup_train,
    down_train,
):
    count = prompts.shape[0]
    tok = prompts.shape[1]
    width = prompts.shape[2]
    groups = lax.axis_size("seq")

    blocks = lax.axis_size("req")
    w_qkv = gather_weights(qkv_train)
    w_gu = gather_weights(gateup_train)
    down_rows = down_train.shape[0]
    padded_rows = -(-down_rows // 16) * 16
    down_piece = jnp.pad(down_train.astype(jnp.bfloat16), ((0, padded_rows - down_rows), (0, 0)))
    stacked = jnp.concatenate([down_piece, out_train.astype(jnp.bfloat16)], axis=0)
    rest = lax.all_gather(stacked[None], ("req", "seq"), axis=0, tiled=True)
    rest = rest.reshape(blocks, groups, stacked.shape[0], stacked.shape[1])
    w_down = rest[:, :, :padded_rows].reshape(blocks, -1, down_train.shape[1])
    w_out = rest[:, :, padded_rows:].reshape(blocks, -1, out_train.shape[1])

    places = lax.axis_index("seq") * tok + jnp.arange(tok, dtype=jnp.int32)
    positions = jnp.tile(places, count).astype(jnp.float32)

    initials = lax.axis_index("req") * count + jnp.arange(count, dtype=jnp.int32)
    own_len = jnp.take(lengths, initials)
    valid = (places[None, :] < own_len[:, None]).astype(jnp.float32).reshape(count * tok, 1)
    rows = prompts.reshape(count * tok, width)
    normed = rms_scale(rows, norm_attn).astype(jnp.bfloat16)
    qkv = apply(normed, w_qkv) + qkv_bias
    query = rotate(qkv[:, :width], positions).astype(jnp.bfloat16)
    keys = rotate(qkv[:, width : 2 * width], positions).astype(jnp.bfloat16)
    values = qkv[:, 2 * width :].astype(jnp.bfloat16)
    per_device = count * HEADS // groups

    def to_pairs(array):
        paired = array.reshape(count, tok, HEADS, HD).transpose(0, 2, 1, 3)
        return paired.reshape(groups, per_device, tok, HD)

    gathered = attend_xla(
        (
            lax.all_to_all(to_pairs(query), "seq", split_axis=0, concat_axis=2, tiled=True),
            lax.all_to_all(to_pairs(keys), "seq", split_axis=0, concat_axis=2, tiled=True),
            lax.all_to_all(to_pairs(values), "seq", split_axis=0, concat_axis=2, tiled=True),
        )
    )
    returned = lax.all_to_all(gathered, "seq", split_axis=2, concat_axis=0, tiled=True)
    attended = (
        returned.reshape(count, HEADS, tok, HD).transpose(0, 2, 1, 3).reshape(count * tok, width)
    )
    mid = rows.astype(jnp.float32) + apply(attended, w_out)
    own_keep = valid.astype(jnp.bfloat16)
    cached = jnp.concatenate([keys * own_keep, values * own_keep], axis=1).reshape(count, tok, 2 * width)
    cached, mid = lax.optimization_barrier((cached, mid))
    everyone = lax.all_gather(cached, "req", axis=0, tiled=True)
    normed2 = rms_scale(mid, norm_mlp).astype(jnp.bfloat16)
    both = apply_blocks(normed2, w_gu)
    half = len(both) // 2
    hidden = jnp.concatenate(
        [(jax.nn.silu(both[r]) * both[half + r]).astype(jnp.bfloat16) for r in range(half)], axis=1
    )
    hidden = jnp.pad(
        hidden.reshape(count * tok, groups, down_rows), ((0, 0), (0, 0), (0, padded_rows - down_rows))
    ).reshape(count * tok, -1)
    states = (
        ((mid + apply(hidden, w_down)) * valid).astype(jnp.bfloat16).reshape(count, tok, width)
    )

    chosen = jnp.take(perm, initials)
    dealt = jnp.take(everyone, chosen, axis=0)
    key_cache = dealt[:, :, :width]
    value_cache = dealt[:, :, width:]
    return (states, key_cache, value_cache)


def solution(mesh):
    placed = (
        P("req", "seq", None),
        P(),
        P(),
        P(),
        P(),
        P("seq", "req"),
        P(),
        P("seq", "req"),
        P("seq", "req"),
        P("seq", "req"),
    )
    return jax.shard_map(
        local,
        mesh=mesh,
        in_specs=placed,
        out_specs=(P("req", "seq", None), P("req", "seq", None), P("req", "seq", None)),
        check_vma=False,
    )
```

```python
import jax
import jax.numpy as jnp
from jax import lax
from jax.sharding import PartitionSpec as P

HEADS = 16
HD = 64


def rms_scale(rows, gain):
    rows = rows.astype(jnp.float32)
    return rows * lax.rsqrt(jnp.mean(rows * rows, axis=-1, keepdims=True) + 1e-06) * gain


def rotate(block, positions):
    half = HD // 2
    count = block.shape[0]
    freqs = jnp.power(1000000.0, -2.0 * jnp.arange(half).astype(jnp.float32) / HD)
    angle = positions[:, None] * freqs[None, :]
    cosine = jnp.cos(angle)[:, None, :]
    sine = jnp.sin(angle)[:, None, :]
    heads = block.reshape(count, -1, HD)
    first = heads[:, :, :half]
    second = heads[:, :, half:]
    turned = jnp.concatenate(
        [first * cosine - second * sine, second * cosine + first * sine], axis=-1
    )
    return turned.reshape(count, -1)


def apply_blocks(inputs, gathered):
    return [jnp.dot(inputs, gathered[r], preferred_element_type=jnp.float32) for r in range(gathered.shape[0])]


def apply(inputs, gathered):
    return jnp.concatenate(apply_blocks(inputs, gathered), axis=1)


def attend_xla(items):
    query, keys, values = items
    length = query.shape[2]
    block = min(512, length)
    scale = HD ** (-0.5)
    pieces = []
    for start in range(0, length, block):
        reach = start + block
        q_block = query[:, :, start:reach]
        scores = (
            jnp.einsum("bnid,bnjd->bnij", q_block, keys[:, :, :reach], preferred_element_type=jnp.float32)
            * scale
        )
        causal = jnp.arange(reach)[None, :] <= (start + jnp.arange(block))[:, None]
        scores = jnp.where(causal[None, None], scores, -1e30)
        top = jnp.max(scores, axis=-1, keepdims=True)
        expo = jnp.exp(scores - top)
        probs = (expo / jnp.sum(expo, axis=-1, keepdims=True)).astype(jnp.bfloat16)
        out = jnp.einsum("bnij,bnjd->bnid", probs, values[:, :, :reach], preferred_element_type=jnp.float32)
        pieces.append(out.astype(jnp.bfloat16))
    return jnp.concatenate(pieces, axis=2)


def gather_weights(piece, rows=None):
    piece = piece.astype(jnp.bfloat16)
    if rows is not None and rows != piece.shape[0]:
        piece = jnp.pad(piece, ((0, rows - piece.shape[0]), (0, 0)))
    whole = lax.all_gather(piece[None], ("req", "seq"), axis=0, tiled=True)
    return whole.reshape(lax.axis_size("req"), -1, piece.shape[1])


def local(
    prompts,
    perm,
    lengths,
    norm_attn,
    norm_mlp,
    qkv_train,
    qkv_bias,
    out_train,
    gateup_train,
    down_train,
):
    count = prompts.shape[0]
    tok = prompts.shape[1]
    width = prompts.shape[2]
    groups = lax.axis_size("seq")

    blocks = lax.axis_size("req")
    w_qkv = gather_weights(qkv_train)
    w_gu = gather_weights(gateup_train)
    down_rows = down_train.shape[0]
    padded_rows = -(-down_rows // 16) * 16
    down_piece = jnp.pad(down_train.astype(jnp.bfloat16), ((0, padded_rows - down_rows), (0, 0)))
    stacked = jnp.concatenate([down_piece, out_train.astype(jnp.bfloat16)], axis=0)
    rest = lax.all_gather(stacked[None], ("req", "seq"), axis=0, tiled=True)
    rest = rest.reshape(blocks, groups, stacked.shape[0], stacked.shape[1])
    w_down = rest[:, :, :padded_rows].reshape(blocks, -1, down_train.shape[1])
    w_out = rest[:, :, padded_rows:].reshape(blocks, -1, out_train.shape[1])

    places = lax.axis_index("seq") * tok + jnp.arange(tok, dtype=jnp.int32)
    positions = jnp.tile(places, count).astype(jnp.float32)

    initials = lax.axis_index("req") * count + jnp.arange(count, dtype=jnp.int32)
    own_len = jnp.take(lengths, initials)
    valid = (places[None, :] < own_len[:, None]).astype(jnp.float32).reshape(count * tok, 1)
    rows = prompts.reshape(count * tok, width)
    normed = rms_scale(rows, norm_attn).astype(jnp.bfloat16)
    qkv = apply(normed, w_qkv) + qkv_bias
    query = rotate(qkv[:, :width], positions).astype(jnp.bfloat16)
    keys = rotate(qkv[:, width : 2 * width], positions).astype(jnp.bfloat16)
    values = qkv[:, 2 * width :].astype(jnp.bfloat16)
    per_device = count * HEADS // groups

    own_keep = valid.astype(jnp.bfloat16)
    cached = jnp.concatenate([keys * own_keep, values * own_keep], axis=1).reshape(count, tok, 2 * width)
    copies = jnp.broadcast_to(cached[None], (blocks,) + cached.shape)
    everyone = lax.all_to_all(copies, "req", 0, 0, tiled=True).reshape(blocks * count, tok, 2 * width)

    def to_pairs(array):
        paired = array.reshape(count, tok, HEADS, HD).transpose(0, 2, 1, 3)
        return paired.reshape(groups, per_device, tok, HD)

    gathered = attend_xla(
        (
            lax.all_to_all(to_pairs(query), "seq", split_axis=0, concat_axis=2, tiled=True),
            lax.all_to_all(to_pairs(keys), "seq", split_axis=0, concat_axis=2, tiled=True),
            lax.all_to_all(to_pairs(values), "seq", split_axis=0, concat_axis=2, tiled=True),
        )
    )
    returned = lax.all_to_all(gathered, "seq", split_axis=2, concat_axis=0, tiled=True)
    attended = (
        returned.reshape(count, HEADS, tok, HD).transpose(0, 2, 1, 3).reshape(count * tok, width)
    )
    mid = rows.astype(jnp.float32) + apply(attended, w_out)
    normed2 = rms_scale(mid, norm_mlp).astype(jnp.bfloat16)
    both = apply_blocks(normed2, w_gu)
    half = len(both) // 2
    hidden = jnp.concatenate(
        [(jax.nn.silu(both[r]) * both[half + r]).astype(jnp.bfloat16) for r in range(half)], axis=1
    )
    hidden = jnp.pad(
        hidden.reshape(count * tok, groups, down_rows), ((0, 0), (0, 0), (0, padded_rows - down_rows))
    ).reshape(count * tok, -1)
    states = (
        ((mid + apply(hidden, w_down)) * valid).astype(jnp.bfloat16).reshape(count, tok, width)
    )

    chosen = jnp.take(perm, initials)
    dealt = jnp.take(everyone, chosen, axis=0)
    key_cache = dealt[:, :, :width]
    value_cache = dealt[:, :, width:]
    return (states, key_cache, value_cache)


def solution(mesh):
    placed = (
        P("req", "seq", None),
        P(),
        P(),
        P(),
        P(),
        P("seq", "req"),
        P(),
        P("seq", "req"),
        P("seq", "req"),
        P("seq", "req"),
    )
    return jax.shard_map(
        local,
        mesh=mesh,
        in_specs=placed,
        out_specs=(P("req", "seq", None), P("req", "seq", None), P("req", "seq", None)),
        check_vma=False,
    )
```

```python
import jax
import jax.numpy as jnp
from jax import lax
from jax.sharding import PartitionSpec as P

HEADS = 16
HD = 64


def rms_scale(rows, gain):
    rows = rows.astype(jnp.float32)
    return rows * lax.rsqrt(jnp.mean(rows * rows, axis=-1, keepdims=True) + 1e-06) * gain


def rotate(block, positions):
    half = HD // 2
    count = block.shape[0]
    freqs = jnp.power(1000000.0, -2.0 * jnp.arange(half).astype(jnp.float32) / HD)
    angle = positions[:, None] * freqs[None, :]
    cosine = jnp.cos(angle)[:, None, :]
    sine = jnp.sin(angle)[:, None, :]
    heads = block.reshape(count, -1, HD)
    first = heads[:, :, :half]
    second = heads[:, :, half:]
    turned = jnp.concatenate(
        [first * cosine - second * sine, second * cosine + first * sine], axis=-1
    )
    return turned.reshape(count, -1)


def apply_blocks(inputs, gathered):
    return [jnp.dot(inputs, gathered[r], preferred_element_type=jnp.float32) for r in range(gathered.shape[0])]


def apply(inputs, gathered):
    return jnp.concatenate(apply_blocks(inputs, gathered), axis=1)


def attend_xla(items):
    query, keys, values = items
    length = query.shape[2]
    block = min(512, length)
    scale = HD ** (-0.5)
    pieces = []
    for start in range(0, length, block):
        reach = start + block
        q_block = query[:, :, start:reach]
        scores = (
            jnp.einsum("bnid,bnjd->bnij", q_block, keys[:, :, :reach], preferred_element_type=jnp.float32)
            * scale
        )
        causal = jnp.arange(reach)[None, :] <= (start + jnp.arange(block))[:, None]
        scores = jnp.where(causal[None, None], scores, -1e30)
        top = jnp.max(scores, axis=-1, keepdims=True)
        expo = jnp.exp(scores - top)
        probs = (expo / jnp.sum(expo, axis=-1, keepdims=True)).astype(jnp.bfloat16)
        out = jnp.einsum("bnij,bnjd->bnid", probs, values[:, :, :reach], preferred_element_type=jnp.float32)
        pieces.append(out.astype(jnp.bfloat16))
    return jnp.concatenate(pieces, axis=2)


def gather_weights(piece, rows=None):
    piece = piece.astype(jnp.bfloat16)
    if rows is not None and rows != piece.shape[0]:
        piece = jnp.pad(piece, ((0, rows - piece.shape[0]), (0, 0)))
    whole = lax.all_gather(piece[None], ("req", "seq"), axis=0, tiled=True)
    return whole.reshape(lax.axis_size("req"), -1, piece.shape[1])


def local(
    prompts,
    perm,
    lengths,
    norm_attn,
    norm_mlp,
    qkv_train,
    qkv_bias,
    out_train,
    gateup_train,
    down_train,
):
    count = prompts.shape[0]
    tok = prompts.shape[1]
    width = prompts.shape[2]
    groups = lax.axis_size("seq")

    blocks = lax.axis_size("req")
    qkv_cols = lax.all_gather(qkv_train.astype(jnp.bfloat16), "req", axis=1, tiled=True)
    w_qkv = lax.all_gather(qkv_cols, "seq", axis=0, tiled=True)
    w_gu = gather_weights(gateup_train)
    down_rows = down_train.shape[0]
    padded_rows = -(-down_rows // 16) * 16
    down_piece = jnp.pad(down_train.astype(jnp.bfloat16), ((0, padded_rows - down_rows), (0, 0)))
    stacked = jnp.concatenate([down_piece, out_train.astype(jnp.bfloat16)], axis=0)
    rest = lax.all_gather(stacked[None], ("req", "seq"), axis=0, tiled=True)
    rest = rest.reshape(blocks, groups, stacked.shape[0], stacked.shape[1])
    w_down = rest[:, :, :padded_rows].reshape(blocks, -1, down_train.shape[1])
    w_out = rest[:, :, padded_rows:].reshape(blocks, -1, out_train.shape[1])

    places = lax.axis_index("seq") * tok + jnp.arange(tok, dtype=jnp.int32)
    positions = jnp.tile(places, count).astype(jnp.float32)

    initials = lax.axis_index("req") * count + jnp.arange(count, dtype=jnp.int32)
    own_len = jnp.take(lengths, initials)
    valid = (places[None, :] < own_len[:, None]).astype(jnp.float32).reshape(count * tok, 1)
    rows = prompts.reshape(count * tok, width)
    normed = rms_scale(rows, norm_attn).astype(jnp.bfloat16)
    qkv = jnp.dot(normed, w_qkv, preferred_element_type=jnp.float32) + qkv_bias
    query = rotate(qkv[:, :width], positions).astype(jnp.bfloat16)
    keys = rotate(qkv[:, width : 2 * width], positions).astype(jnp.bfloat16)
    values = qkv[:, 2 * width :].astype(jnp.bfloat16)
    per_device = count * HEADS // groups

    def to_pairs(array):
        paired = array.reshape(count, tok, HEADS, HD).transpose(0, 2, 1, 3)
        return paired.reshape(groups, per_device, tok, HD)

    gathered = attend_xla(
        (
            lax.all_to_all(to_pairs(query), "seq", split_axis=0, concat_axis=2, tiled=True),
            lax.all_to_all(to_pairs(keys), "seq", split_axis=0, concat_axis=2, tiled=True),
            lax.all_to_all(to_pairs(values), "seq", split_axis=0, concat_axis=2, tiled=True),
        )
    )
    returned = lax.all_to_all(gathered, "seq", split_axis=2, concat_axis=0, tiled=True)
    attended = (
        returned.reshape(count, HEADS, tok, HD).transpose(0, 2, 1, 3).reshape(count * tok, width)
    )
    mid = rows.astype(jnp.float32) + apply(attended, w_out)
    own_keep = valid.astype(jnp.bfloat16)
    cached = jnp.concatenate([keys * own_keep, values * own_keep], axis=1).reshape(count, tok, 2 * width)
    cached, mid = lax.optimization_barrier((cached, mid))
    everyone = lax.all_gather(cached, "req", axis=0, tiled=True)
    normed2 = rms_scale(mid, norm_mlp).astype(jnp.bfloat16)
    both = apply_blocks(normed2, w_gu)
    half = len(both) // 2
    hidden = jnp.concatenate(
        [(jax.nn.silu(both[r]) * both[half + r]).astype(jnp.bfloat16) for r in range(half)], axis=1
    )
    hidden = jnp.pad(
        hidden.reshape(count * tok, groups, down_rows), ((0, 0), (0, 0), (0, padded_rows - down_rows))
    ).reshape(count * tok, -1)
    states = (
        ((mid + apply(hidden, w_down)) * valid).astype(jnp.bfloat16).reshape(count, tok, width)
    )

    chosen = jnp.take(perm, initials)
    dealt = jnp.take(everyone, chosen, axis=0)
    key_cache = dealt[:, :, :width]
    value_cache = dealt[:, :, width:]
    return (states, key_cache, value_cache)


def solution(mesh):
    placed = (
        P("req", "seq", None),
        P(),
        P(),
        P(),
        P(),
        P("seq", "req"),
        P(),
        P("seq", "req"),
        P("seq", "req"),
        P("seq", "req"),
    )
    return jax.shard_map(
        local,
        mesh=mesh,
        in_specs=placed,
        out_specs=(P("req", "seq", None), P("req", "seq", None), P("req", "seq", None)),
        check_vma=False,
    )
```

```python
import jax
import jax.numpy as jnp
from jax import lax
from jax.sharding import PartitionSpec as P

HEADS = 16
HD = 64


def rms_scale(rows, gain):
    rows = rows.astype(jnp.float32)
    return rows * lax.rsqrt(jnp.mean(rows * rows, axis=-1, keepdims=True) + 1e-06) * gain


def rotate(block, positions):
    half = HD // 2
    count = block.shape[0]
    freqs = jnp.power(1000000.0, -2.0 * jnp.arange(half).astype(jnp.float32) / HD)
    angle = positions[:, None] * freqs[None, :]
    cosine = jnp.cos(angle)[:, None, :]
    sine = jnp.sin(angle)[:, None, :]
    heads = block.reshape(count, -1, HD)
    first = heads[:, :, :half]
    second = heads[:, :, half:]
    turned = jnp.concatenate(
        [first * cosine - second * sine, second * cosine + first * sine], axis=-1
    )
    return turned.reshape(count, -1)


def apply_blocks(inputs, gathered):
    return [jnp.dot(inputs, gathered[r], preferred_element_type=jnp.float32) for r in range(gathered.shape[0])]


def apply(inputs, gathered):
    return jnp.concatenate(apply_blocks(inputs, gathered), axis=1)


def attend_xla(items):
    query, keys, values = items
    length = query.shape[2]
    block = min(512, length)
    scale = HD ** (-0.5)
    pieces = []
    for start in range(0, length, block):
        reach = start + block
        q_block = query[:, :, start:reach]
        scores = (
            jnp.einsum("bnid,bnjd->bnij", q_block, keys[:, :, :reach], preferred_element_type=jnp.float32)
            * scale
        )
        causal = jnp.arange(reach)[None, :] <= (start + jnp.arange(block))[:, None]
        scores = jnp.where(causal[None, None], scores, -1e30)
        top = jnp.max(scores, axis=-1, keepdims=True)
        expo = jnp.exp(scores - top)
        probs = (expo / jnp.sum(expo, axis=-1, keepdims=True)).astype(jnp.bfloat16)
        out = jnp.einsum("bnij,bnjd->bnid", probs, values[:, :, :reach], preferred_element_type=jnp.float32)
        pieces.append(out.astype(jnp.bfloat16))
    return jnp.concatenate(pieces, axis=2)


def gather_weights(piece, rows=None):
    piece = piece.astype(jnp.bfloat16)
    if rows is not None and rows != piece.shape[0]:
        piece = jnp.pad(piece, ((0, rows - piece.shape[0]), (0, 0)))
    whole = lax.all_gather(piece[None], ("req", "seq"), axis=0, tiled=True)
    return whole.reshape(lax.axis_size("req"), -1, piece.shape[1])


def local(
    prompts,
    perm,
    lengths,
    norm_attn,
    norm_mlp,
    qkv_train,
    qkv_bias,
    out_train,
    gateup_train,
    down_train,
):
    count = prompts.shape[0]
    tok = prompts.shape[1]
    width = prompts.shape[2]
    groups = lax.axis_size("seq")

    blocks = lax.axis_size("req")
    qkv_cols = lax.all_gather(qkv_train.astype(jnp.bfloat16), "req", axis=1, tiled=True)
    w_qkv = lax.all_gather(qkv_cols, "seq", axis=0, tiled=True)
    w_gu = gather_weights(gateup_train)
    down_rows = down_train.shape[0]
    padded_rows = -(-down_rows // 16) * 16
    down_piece = jnp.pad(down_train.astype(jnp.bfloat16), ((0, padded_rows - down_rows), (0, 0)))
    stacked = jnp.concatenate([down_piece, out_train.astype(jnp.bfloat16)], axis=0)
    rest = lax.all_gather(stacked[None], ("req", "seq"), axis=0, tiled=True)
    rest = rest.reshape(blocks, groups, stacked.shape[0], stacked.shape[1])
    w_down = rest[:, :, :padded_rows].reshape(blocks, -1, down_train.shape[1])
    w_out = rest[:, :, padded_rows:].reshape(blocks, -1, out_train.shape[1])

    places = lax.axis_index("seq") * tok + jnp.arange(tok, dtype=jnp.int32)
    positions = jnp.tile(places, count).astype(jnp.float32)

    initials = lax.axis_index("req") * count + jnp.arange(count, dtype=jnp.int32)
    own_len = jnp.take(lengths, initials)
    valid = (places[None, :] < own_len[:, None]).astype(jnp.float32).reshape(count * tok, 1)
    rows = prompts.reshape(count * tok, width)
    normed = rms_scale(rows, norm_attn).astype(jnp.bfloat16)
    qkv = jnp.dot(normed, w_qkv, preferred_element_type=jnp.float32) + qkv_bias
    query = rotate(qkv[:, :width], positions).astype(jnp.bfloat16)
    keys = rotate(qkv[:, width : 2 * width], positions).astype(jnp.bfloat16)
    values = qkv[:, 2 * width :].astype(jnp.bfloat16)
    per_device = count * HEADS // groups

    def to_pairs(array):
        paired = array.reshape(count, tok, HEADS, HD).transpose(0, 2, 1, 3)
        return paired.reshape(groups, per_device, tok, HD)

    gathered = attend_xla(
        (
            lax.all_to_all(to_pairs(query), "seq", split_axis=0, concat_axis=2, tiled=True),
            lax.all_to_all(to_pairs(keys), "seq", split_axis=0, concat_axis=2, tiled=True),
            lax.all_to_all(to_pairs(values), "seq", split_axis=0, concat_axis=2, tiled=True),
        )
    )
    own_keep = valid.astype(jnp.bfloat16)
    cached = jnp.concatenate([keys * own_keep, values * own_keep], axis=1).reshape(count, tok, 2 * width)
    cached, gathered, w_gu = lax.optimization_barrier((cached, gathered, w_gu))
    everyone = lax.all_gather(cached, "req", axis=0, tiled=True)
    returned = lax.all_to_all(gathered, "seq", split_axis=2, concat_axis=0, tiled=True)
    attended = (
        returned.reshape(count, HEADS, tok, HD).transpose(0, 2, 1, 3).reshape(count * tok, width)
    )
    mid = rows.astype(jnp.float32) + apply(attended, w_out)
    normed2 = rms_scale(mid, norm_mlp).astype(jnp.bfloat16)
    both = apply_blocks(normed2, w_gu)
    half = len(both) // 2
    hidden = jnp.concatenate(
        [(jax.nn.silu(both[r]) * both[half + r]).astype(jnp.bfloat16) for r in range(half)], axis=1
    )
    hidden = jnp.pad(
        hidden.reshape(count * tok, groups, down_rows), ((0, 0), (0, 0), (0, padded_rows - down_rows))
    ).reshape(count * tok, -1)
    states = (
        ((mid + apply(hidden, w_down)) * valid).astype(jnp.bfloat16).reshape(count, tok, width)
    )

    chosen = jnp.take(perm, initials)
    dealt = jnp.take(everyone, chosen, axis=0)
    key_cache = dealt[:, :, :width]
    value_cache = dealt[:, :, width:]
    return (states, key_cache, value_cache)


def solution(mesh):
    placed = (
        P("req", "seq", None),
        P(),
        P(),
        P(),
        P(),
        P("seq", "req"),
        P(),
        P("seq", "req"),
        P("seq", "req"),
        P("seq", "req"),
    )
    return jax.shard_map(
        local,
        mesh=mesh,
        in_specs=placed,
        out_specs=(P("req", "seq", None), P("req", "seq", None), P("req", "seq", None)),
        check_vma=False,
    )
```

```python
import jax
import jax.numpy as jnp
from jax import lax
from jax.sharding import PartitionSpec as P

HEADS = 16
HD = 64


def rms_scale(rows, gain):
    rows = rows.astype(jnp.float32)
    return rows * lax.rsqrt(jnp.mean(rows * rows, axis=-1, keepdims=True) + 1e-06) * gain


def rotate(block, positions):
    half = HD // 2
    count = block.shape[0]
    freqs = jnp.power(1000000.0, -2.0 * jnp.arange(half).astype(jnp.float32) / HD)
    angle = positions[:, None] * freqs[None, :]
    cosine = jnp.cos(angle)[:, None, :]
    sine = jnp.sin(angle)[:, None, :]
    heads = block.reshape(count, -1, HD)
    first = heads[:, :, :half]
    second = heads[:, :, half:]
    turned = jnp.concatenate(
        [first * cosine - second * sine, second * cosine + first * sine], axis=-1
    )
    return turned.reshape(count, -1)


def apply_blocks(inputs, gathered):
    return [jnp.dot(inputs, gathered[r], preferred_element_type=jnp.float32) for r in range(gathered.shape[0])]


def apply(inputs, gathered):
    return jnp.concatenate(apply_blocks(inputs, gathered), axis=1)


def attend_xla(items):
    query, keys, values = items
    length = query.shape[2]
    block = min(512, length)
    scale = HD ** (-0.5)
    pieces = []
    for start in range(0, length, block):
        reach = start + block
        q_block = query[:, :, start:reach]
        scores = (
            jnp.einsum("bnid,bnjd->bnij", q_block, keys[:, :, :reach], preferred_element_type=jnp.float32)
            * scale
        )
        causal = jnp.arange(reach)[None, :] <= (start + jnp.arange(block))[:, None]
        scores = jnp.where(causal[None, None], scores, -1e30)
        top = jnp.max(scores, axis=-1, keepdims=True)
        expo = jnp.exp(scores - top)
        probs = (expo / jnp.sum(expo, axis=-1, keepdims=True)).astype(jnp.bfloat16)
        out = jnp.einsum("bnij,bnjd->bnid", probs, values[:, :, :reach], preferred_element_type=jnp.float32)
        pieces.append(out.astype(jnp.bfloat16))
    return jnp.concatenate(pieces, axis=2)


def gather_weights(piece, rows=None):
    piece = piece.astype(jnp.bfloat16)
    if rows is not None and rows != piece.shape[0]:
        piece = jnp.pad(piece, ((0, rows - piece.shape[0]), (0, 0)))
    whole = lax.all_gather(piece[None], ("req", "seq"), axis=0, tiled=True)
    return whole.reshape(lax.axis_size("req"), -1, piece.shape[1])


def local(
    prompts,
    perm,
    lengths,
    norm_attn,
    norm_mlp,
    qkv_train,
    qkv_bias,
    out_train,
    gateup_train,
    down_train,
):
    count = prompts.shape[0]
    tok = prompts.shape[1]
    width = prompts.shape[2]
    groups = lax.axis_size("seq")

    blocks = lax.axis_size("req")
    qkv_cols = lax.all_gather(qkv_train.astype(jnp.bfloat16), "req", axis=1, tiled=True)
    w_qkv = lax.all_gather(qkv_cols, "seq", axis=0, tiled=True)
    w_gu = gather_weights(gateup_train)
    down_rows = down_train.shape[0]
    padded_rows = down_rows
    stacked = jnp.concatenate([down_train.astype(jnp.bfloat16), out_train.astype(jnp.bfloat16)], axis=0)
    rest = lax.all_gather(stacked[None], ("req", "seq"), axis=0, tiled=True)
    rest = rest.reshape(blocks, groups, stacked.shape[0], stacked.shape[1])
    w_down = rest[:, :, :padded_rows].reshape(blocks, -1, down_train.shape[1])
    w_out = rest[:, :, padded_rows:].reshape(blocks, -1, out_train.shape[1])

    places = lax.axis_index("seq") * tok + jnp.arange(tok, dtype=jnp.int32)
    positions = jnp.tile(places, count).astype(jnp.float32)

    initials = lax.axis_index("req") * count + jnp.arange(count, dtype=jnp.int32)
    own_len = jnp.take(lengths, initials)
    valid = (places[None, :] < own_len[:, None]).astype(jnp.float32).reshape(count * tok, 1)
    rows = prompts.reshape(count * tok, width)
    normed = rms_scale(rows, norm_attn).astype(jnp.bfloat16)
    qkv = jnp.dot(normed, w_qkv, preferred_element_type=jnp.float32) + qkv_bias
    query = rotate(qkv[:, :width], positions).astype(jnp.bfloat16)
    keys = rotate(qkv[:, width : 2 * width], positions).astype(jnp.bfloat16)
    values = qkv[:, 2 * width :].astype(jnp.bfloat16)
    per_device = count * HEADS // groups

    def to_pairs(array):
        paired = array.reshape(count, tok, HEADS, HD).transpose(0, 2, 1, 3)
        return paired.reshape(groups, per_device, tok, HD)

    gathered = attend_xla(
        (
            lax.all_to_all(to_pairs(query), "seq", split_axis=0, concat_axis=2, tiled=True),
            lax.all_to_all(to_pairs(keys), "seq", split_axis=0, concat_axis=2, tiled=True),
            lax.all_to_all(to_pairs(values), "seq", split_axis=0, concat_axis=2, tiled=True),
        )
    )
    own_keep = valid.astype(jnp.bfloat16)
    cached = jnp.concatenate([keys * own_keep, values * own_keep], axis=1).reshape(count, tok, 2 * width)
    cached, gathered, w_gu = lax.optimization_barrier((cached, gathered, w_gu))
    everyone = lax.all_gather(cached, "req", axis=0, tiled=True)
    returned = lax.all_to_all(gathered, "seq", split_axis=2, concat_axis=0, tiled=True)
    attended = (
        returned.reshape(count, HEADS, tok, HD).transpose(0, 2, 1, 3).reshape(count * tok, width)
    )
    mid = rows.astype(jnp.float32) + apply(attended, w_out)
    normed2 = rms_scale(mid, norm_mlp).astype(jnp.bfloat16)
    both = apply_blocks(normed2, w_gu)
    half = len(both) // 2
    hidden = jnp.concatenate(
        [(jax.nn.silu(both[r]) * both[half + r]).astype(jnp.bfloat16) for r in range(half)], axis=1
    )
    states = (
        ((mid + apply(hidden, w_down)) * valid).astype(jnp.bfloat16).reshape(count, tok, width)
    )

    chosen = jnp.take(perm, initials)
    dealt = jnp.take(everyone, chosen, axis=0)
    key_cache = dealt[:, :, :width]
    value_cache = dealt[:, :, width:]
    return (states, key_cache, value_cache)


def solution(mesh):
    placed = (
        P("req", "seq", None),
        P(),
        P(),
        P(),
        P(),
        P("seq", "req"),
        P(),
        P("seq", "req"),
        P("seq", "req"),
        P("seq", "req"),
    )
    return jax.shard_map(
        local,
        mesh=mesh,
        in_specs=placed,
        out_specs=(P("req", "seq", None), P("req", "seq", None), P("req", "seq", None)),
        check_vma=False,
    )
```

```python
import jax
import jax.numpy as jnp
from jax import lax
from jax.sharding import PartitionSpec as P

HEADS = 16
HD = 64


def rms_scale(rows, gain):
    rows = rows.astype(jnp.float32)
    return rows * lax.rsqrt(jnp.mean(rows * rows, axis=-1, keepdims=True) + 1e-06) * gain


def rotate(block, positions):
    half = HD // 2
    count = block.shape[0]
    freqs = jnp.power(1000000.0, -2.0 * jnp.arange(half).astype(jnp.float32) / HD)
    angle = positions[:, None] * freqs[None, :]
    cosine = jnp.cos(angle)[:, None, :]
    sine = jnp.sin(angle)[:, None, :]
    heads = block.reshape(count, -1, HD)
    first = heads[:, :, :half]
    second = heads[:, :, half:]
    turned = jnp.concatenate(
        [first * cosine - second * sine, second * cosine + first * sine], axis=-1
    )
    return turned.reshape(count, -1)


def apply_blocks(inputs, gathered):
    return [jnp.dot(inputs, gathered[r], preferred_element_type=jnp.float32) for r in range(gathered.shape[0])]


def apply(inputs, gathered):
    return jnp.concatenate(apply_blocks(inputs, gathered), axis=1)


def attend_xla(items):
    query, keys, values = items
    length = query.shape[2]
    block = min(512, length)
    scale = HD ** (-0.5)
    pieces = []
    for start in range(0, length, block):
        reach = start + block
        q_block = query[:, :, start:reach]
        scores = (
            jnp.einsum("bnid,bnjd->bnij", q_block, keys[:, :, :reach], preferred_element_type=jnp.float32)
            * scale
        )
        causal = jnp.arange(reach)[None, :] <= (start + jnp.arange(block))[:, None]
        scores = jnp.where(causal[None, None], scores, -1e30)
        top = jnp.max(scores, axis=-1, keepdims=True)
        expo = jnp.exp(scores - top)
        probs = (expo / jnp.sum(expo, axis=-1, keepdims=True)).astype(jnp.bfloat16)
        out = jnp.einsum("bnij,bnjd->bnid", probs, values[:, :, :reach], preferred_element_type=jnp.float32)
        pieces.append(out.astype(jnp.bfloat16))
    return jnp.concatenate(pieces, axis=2)


def gather_weights(piece, rows=None):
    piece = piece.astype(jnp.bfloat16)
    if rows is not None and rows != piece.shape[0]:
        piece = jnp.pad(piece, ((0, rows - piece.shape[0]), (0, 0)))
    whole = lax.all_gather(piece[None], ("req", "seq"), axis=0, tiled=True)
    return whole.reshape(lax.axis_size("req"), -1, piece.shape[1])


def local(
    prompts,
    perm,
    lengths,
    norm_attn,
    norm_mlp,
    qkv_train,
    qkv_bias,
    out_train,
    gateup_train,
    down_train,
):
    count = prompts.shape[0]
    tok = prompts.shape[1]
    width = prompts.shape[2]
    groups = lax.axis_size("seq")

    blocks = lax.axis_size("req")
    qkv_cols = lax.all_gather(qkv_train.astype(jnp.bfloat16), "req", axis=1, tiled=True)
    w_qkv = lax.all_gather(qkv_cols, "seq", axis=0, tiled=True)
    w_gu = gather_weights(gateup_train)
    down_rows = down_train.shape[0]
    padded_rows = down_rows
    out_rows = out_train.shape[0]
    stacked = jnp.concatenate([out_train.astype(jnp.bfloat16), down_train.astype(jnp.bfloat16)], axis=0)
    rest = lax.all_gather(stacked[None], ("req", "seq"), axis=0, tiled=True)
    rest = rest.reshape(blocks, groups, stacked.shape[0], stacked.shape[1])
    w_out = rest[:, :, :out_rows].reshape(blocks, -1, out_train.shape[1])
    w_down = rest[:, :, out_rows:].reshape(blocks, -1, down_train.shape[1])

    places = lax.axis_index("seq") * tok + jnp.arange(tok, dtype=jnp.int32)
    positions = jnp.tile(places, count).astype(jnp.float32)

    initials = lax.axis_index("req") * count + jnp.arange(count, dtype=jnp.int32)
    own_len = jnp.take(lengths, initials)
    valid = (places[None, :] < own_len[:, None]).astype(jnp.float32).reshape(count * tok, 1)
    rows = prompts.reshape(count * tok, width)
    normed = rms_scale(rows, norm_attn).astype(jnp.bfloat16)
    qkv = jnp.dot(normed, w_qkv, preferred_element_type=jnp.float32) + qkv_bias
    query = rotate(qkv[:, :width], positions).astype(jnp.bfloat16)
    keys = rotate(qkv[:, width : 2 * width], positions).astype(jnp.bfloat16)
    values = qkv[:, 2 * width :].astype(jnp.bfloat16)
    per_device = count * HEADS // groups

    def to_pairs(array):
        paired = array.reshape(count, tok, HEADS, HD).transpose(0, 2, 1, 3)
        return paired.reshape(groups, per_device, tok, HD)

    gathered = attend_xla(
        (
            lax.all_to_all(to_pairs(query), "seq", split_axis=0, concat_axis=2, tiled=True),
            lax.all_to_all(to_pairs(keys), "seq", split_axis=0, concat_axis=2, tiled=True),
            lax.all_to_all(to_pairs(values), "seq", split_axis=0, concat_axis=2, tiled=True),
        )
    )
    own_keep = valid.astype(jnp.bfloat16)
    cached = jnp.concatenate([keys * own_keep, values * own_keep], axis=1).reshape(count, tok, 2 * width)
    cached, gathered, w_gu = lax.optimization_barrier((cached, gathered, w_gu))
    everyone = lax.all_gather(cached, "req", axis=0, tiled=True)
    returned = lax.all_to_all(gathered, "seq", split_axis=2, concat_axis=0, tiled=True)
    attended = (
        returned.reshape(count, HEADS, tok, HD).transpose(0, 2, 1, 3).reshape(count * tok, width)
    )
    mid = rows.astype(jnp.float32) + apply(attended, w_out)
    normed2 = rms_scale(mid, norm_mlp).astype(jnp.bfloat16)
    both = apply_blocks(normed2, w_gu)
    half = len(both) // 2
    hidden = jnp.concatenate(
        [(jax.nn.silu(both[r]) * both[half + r]).astype(jnp.bfloat16) for r in range(half)], axis=1
    )
    states = (
        ((mid + apply(hidden, w_down)) * valid).astype(jnp.bfloat16).reshape(count, tok, width)
    )

    chosen = jnp.take(perm, initials)
    dealt = jnp.take(everyone, chosen, axis=0)
    key_cache = dealt[:, :, :width]
    value_cache = dealt[:, :, width:]
    return (states, key_cache, value_cache)


def solution(mesh):
    placed = (
        P("req", "seq", None),
        P(),
        P(),
        P(),
        P(),
        P("seq", "req"),
        P(),
        P("seq", "req"),
        P("seq", "req"),
        P("seq", "req"),
    )
    return jax.shard_map(
        local,
        mesh=mesh,
        in_specs=placed,
        out_specs=(P("req", "seq", None), P("req", "seq", None), P("req", "seq", None)),
        check_vma=False,
    )
```
